128 devices in a mesh: segment: 4 (over x_lo, core), patch: 32 (over x_hi, y, z).
Axes of the slice: x: 4 (x_hi: 2, x_lo: 2; x = x_hi * 2 + x_lo), y: 4, z: 4, core: 2. Of those that a mesh axis runs over, the one named last changes fastest.
Arguments:
- features: bfloat16 [128, 28, 4, 12, 128], P('patch'), may hold values from -6 to 6
- deep_path: bfloat16 [128, 28, 4, 12, 128], P('patch'), may hold values from -6 to 6
- weight_first: bfloat16 [9, 28, 28], replicated, may hold values from -0.375 to 0.375
- bias_first: float32 [28], replicated, may hold values from -3 to 3
- weight_second: bfloat16 [27, 28, 28], replicated, may hold values from -0.21875 to 0.21875
- bias_second: float32 [28], replicated, may hold values from -3 to 3
- weight_third: bfloat16 [27, 28, 56], replicated, may hold values from -0.15625 to 0.15625
- bias_third: float32 [28], replicated, may hold values from -3 to 3
- weight_fourth: bfloat16 [27, 28, 56], replicated, may hold values from -0.15625 to 0.15625
- bias_fourth: float32 [28], replicated, may hold values from -3 to 3
- head_weight: bfloat16 [3, 28], replicated, may hold values from -2 to 2
- head_bias: float32 [3], replicated, may hold values from -3 to 3
- block_first: int32 [128], replicated, may hold values from 0 to 252, as said below
- block_offset: int32 [128], replicated, may hold values from 0 to 3
Outputs:
- blended: float32 [8, 32, 3, 4, 4, 128], P(None, 'patch', None, 'segment')
The draws below stay inside these ranges and needn't reach their ends.
Inputs may be any that keep to these rules, and one draw needn't show every extreme that they name: A patch touches only blocks block_first to block_first + 3, all inside the slab.
All inputs are finite; a program needn't handle non-finite values.
Results may differ from the reference program's by a relative error of at most 0.0022.
Values may be sent and summed in bfloat16 or wider, within the bound.
A program may use at most 64 MiB of HBM per device.

```python
import jax
import jax.numpy as jnp
from jax import lax

C = 28
CD = 56
PZ = 4
PA = 12
PY = 128
CW = 4
CH_DEV = 8
KMAX = 4
PATCHES = 128
OWNERS = 32
NCHUNK = 256


def draw_block_first(key, part):
    top = NCHUNK - KMAX
    key_left, key_right, key_pick = jax.random.split(key, 3)
    left = jax.random.randint(key_left, (PATCHES,), 0, top + 1)
    right = jax.random.randint(key_right, (PATCHES,), 0, top + 1)
    first = jnp.minimum(left, right)
    picks = jax.random.permutation(key_pick, PATCHES)
    index = jnp.arange(PATCHES)
    first = jnp.where(index == picks[0], top, first)
    first = jnp.where(index == picks[1], 0, first)
    return first.astype(jnp.int32)


def place_ends(drawn, rng, low, high):
    spot = [jax.random.randint(jax.random.fold_in(rng, axis), (), 0, length) for axis, length in enumerate(drawn.shape)]
    longest = drawn.shape.index(max(drawn.shape))
    neighbour = spot[:longest] + [(spot[longest] + 1) % drawn.shape[longest]] + spot[longest + 1:]
    return drawn.at[tuple(spot)].set(low).at[tuple(neighbour)].set(high)


def block_levels(stream_key, shape, cuts, low, top_value):
    def one(dim, blocks):
        steps = jax.random.uniform(jax.random.fold_in(jax.random.fold_in(stream_key, 6), dim), (blocks,), jnp.float32, low / len(cuts), top_value / len(cuts))
        return jnp.repeat(jnp.exp(steps), shape[dim] // blocks).reshape((-1,) + (1,) * (len(shape) - dim - 1))

    level = one(*cuts[0])
    for cut in cuts[1:]:
        level = level * one(*cut)
    return level


def bell_draw(rng, extent, scale, reach, cuts=(), kind=jnp.bfloat16):
    entries = jax.random.normal(rng, extent, jnp.float32) * scale
    if len(cuts) > 0:
        entries = block_levels(rng, extent, cuts, -0.22, 0.18) * entries
    return jnp.clip(entries, min=-reach, max=reach).astype(kind)


def setup_inputs(seed: int = 0) -> dict:
    keys = jax.random.split(jax.random.key(seed), 15)
    return {
        "features": bell_draw(keys[0], (PATCHES, C, PZ, PA, PY), 1.0, 6.0, ((0, 32),)),
        "deep_path": bell_draw(keys[1], (PATCHES, C, PZ, PA, PY), 1.0, 6.0, ((0, 32),)),
        "weight_first": bell_draw(keys[2], (9, C, C), (9 * C) ** -0.5, 0.375),
        "bias_first": bell_draw(keys[3], (C,), 0.5, 3.0, (), jnp.float32),
        "weight_second": bell_draw(keys[4], (27, C, C), (27 * C) ** -0.5, 0.21875),
        "bias_second": bell_draw(keys[5], (C,), 0.5, 3.0, (), jnp.float32),
        "weight_third": bell_draw(keys[6], (27, C, CD), (27 * CD) ** -0.5, 0.15625),
        "bias_third": bell_draw(keys[7], (C,), 0.5, 3.0, (), jnp.float32),
        "weight_fourth": bell_draw(keys[8], (27, C, CD), (27 * CD) ** -0.5, 0.15625),
        "bias_fourth": bell_draw(keys[9], (C,), 0.5, 3.0, (), jnp.float32),
        "head_weight": bell_draw(keys[10], (3, C), (C // 4) ** -0.5, 2.0),
        "head_bias": bell_draw(keys[11], (3,), 1.0, 3.0, (), jnp.float32),
        "block_first": draw_block_first(jax.random.fold_in(keys[14], 71), 0),
        "block_offset": place_ends(jax.random.randint(keys[13], (PATCHES,), 0, CW), jax.random.fold_in(keys[13], 1), 0, CW - 1).astype(jnp.int32),
    }


def bump(count):
    place = (jnp.arange(count).astype(jnp.float32) + 0.5) / count
    return jnp.sin(jnp.pi * place) ** 2


def blend_window(depth, along, across):
    return bump(depth)[:, None, None] * bump(along)[None, :, None] * bump(across)[None, None, :]


def convolve_plane(source, kernel):
    depth, along, across = source.shape[1], source.shape[2], source.shape[3]
    padded = jnp.pad(source, ((0, 0), (0, 0), (1, 1), (1, 1))).astype(jnp.float32)
    total = jnp.zeros((kernel.shape[1], depth, along, across), jnp.float32)
    for row_shift in range(3):
        for col_shift in range(3):
            window = padded[:, :, row_shift:row_shift + along, col_shift:col_shift + across]
            total = total + jnp.einsum("oc,czay->ozay", kernel[row_shift * 3 + col_shift].astype(jnp.float32), window)
    return total


def convolve_full(source, kernel):
    depth, along, across = source.shape[1], source.shape[2], source.shape[3]
    padded = jnp.pad(source, ((0, 0), (1, 1), (1, 1), (1, 1))).astype(jnp.float32)
    total = jnp.zeros((kernel.shape[1], depth, along, across), jnp.float32)
    for depth_shift in range(3):
        for row_shift in range(3):
            for col_shift in range(3):
                window = padded[:, depth_shift:depth_shift + depth, row_shift:row_shift + along, col_shift:col_shift + across]
                total = total + jnp.einsum("oc,czay->ozay", kernel[depth_shift * 9 + row_shift * 3 + col_shift].astype(jnp.float32), window)
    return total


def layer(total, bias):
    return jax.nn.relu(total + bias[:, None, None, None]).astype(jnp.bfloat16)


def reference(features, deep_path, weight_first, bias_first, weight_second, bias_second, weight_third, bias_third, weight_fourth, bias_fourth, head_weight, head_bias, block_first, block_offset):
    window = blend_window(PZ, PA, PY)

    def accumulate(slab, items):
        patch_in, deep_in, first_block, offset = items
        first = layer(convolve_plane(patch_in, weight_first), bias_first)
        second = layer(convolve_full(first, weight_second), bias_second)
        third = layer(convolve_full(jnp.concatenate([second, deep_in], axis=0), weight_third), bias_third)
        fourth = layer(convolve_full(jnp.concatenate([third, first], axis=0), weight_fourth), bias_fourth)
        logits = jnp.einsum("oc,czay->ozay", head_weight.astype(jnp.float32), fourth.astype(jnp.float32)) + head_bias[:, None, None, None]
        partial_value = jax.nn.sigmoid(logits) * window
        start = (first_block * CW + offset).astype(jnp.int32)
        zero = jnp.zeros((), jnp.int32)
        current = lax.dynamic_slice(slab, (zero, zero, start, zero), partial_value.shape)
        return lax.dynamic_update_slice(slab, current + partial_value, (zero, zero, start, zero)), None

    slab = jnp.zeros((3, PZ, NCHUNK * CW, PY), jnp.float32)
    slab, unused = lax.scan(accumulate, slab, (features, deep_path, block_first, block_offset))
    return slab.reshape(3, PZ, CH_DEV, OWNERS, CW, PY).transpose(2, 3, 0, 1, 4, 5)
```

```python
import functools
import math

import jax
import jax.numpy as jnp
from jax import lax
from jax.experimental import pallas as pl
from jax.experimental.pallas import tpu as pltpu
from jax.sharding import PartitionSpec as P

bf16 = jnp.bfloat16
f32 = jnp.float32
ROWS = 24


def bump(n, length):
    return math.sin(math.pi * (n + 0.5) / length) ** 2


def conv_kernel(index, feat_hbm, deep_hbm, wf_hbm, ws_hbm, wt_hbm, wo_hbm,
                bf_ref, bs_ref, bt_ref, bo_ref, hw_ref, hb_ref, out_ref,
                fbuf, dbuf, wfb, wsb, wtb, wob, plane, b_feat, b_mid, b_top,
                z_first, z_second, z_third, z_fourth, z_head, sems):
    s = index()
    copies = [
        pltpu.make_async_copy(feat_hbm.at[s], fbuf, sems.at[0]),
        pltpu.make_async_copy(wf_hbm, wfb, sems.at[1]),
        pltpu.make_async_copy(ws_hbm, wsb, sems.at[2]),
        pltpu.make_async_copy(deep_hbm.at[s], dbuf, sems.at[3]),
        pltpu.make_async_copy(wt_hbm, wtb, sems.at[4]),
        pltpu.make_async_copy(wo_hbm, wob, sems.at[5]),
    ]
    for copy in copies:
        copy.start()

    for buf, parts in ((b_feat, 1), (b_mid, 2), (b_top, 2)):
        for side in (0, 13 * 128):
            buf[:, side:side + 128] = jnp.zeros((parts * 384, 128), bf16)
    for z in range(4):
        plane[z * 512 + 448:z * 512 + 512, :] = jnp.zeros((64, 128), f32)
    lane = lax.broadcasted_iota(jnp.int32, (128, 128), 1)
    row = lax.broadcasted_iota(jnp.int32, (128, 128), 0)

    def put(buf, row0, col0, v):
        left = jnp.where(lane > 0, pltpu.roll(v, 1, 1), 0.0)
        right = jnp.where(lane < 127, pltpu.roll(v, 127, 1), 0.0)
        buf[row0:row0 + 128, col0:col0 + 128] = left.astype(bf16)
        buf[row0 + 128:row0 + 256, col0:col0 + 128] = v.astype(bf16)
        buf[row0 + 256:row0 + 384, col0:col0 + 128] = right.astype(bf16)

    def relayout(src, buf, row0):
        for c in range(28):
            for z in range(4):
                base = (z * 32 + c) * 16
                plane[base:base + 12, :] = src[c, z].astype(f32)
        for a in range(12):
            put(buf, row0, (a + 1) * 128, plane[pl.ds(a, 128, stride=16), :])

    def expand(w, dst, parts, full):
        dst[...] = jnp.zeros(dst.shape, bf16)
        for t in range(9):
            da, dy = t // 3, t % 3
            for part in range(parts):
                base = ((da * parts + part) * 3 + dy) * 128
                for zo in range(4):
                    for zi in range(4):
                        if full and abs(zi - zo) > 1 or not full and zi != zo:
                            continue
                        tap = 9 * (zi - zo + 1) + t if full else t
                        dst[zo * 32:zo * 32 + 28, base + zi * 32:base + zi * 32 + 28] = (
                            w[tap, :, part * 28:part * 28 + 28])

    def column(ref):
        lanes = lax.broadcasted_iota(jnp.int32, (128, 28), 1)
        rows = lax.rem(lax.broadcasted_iota(jnp.int32, (128, 28), 0), 32)
        return jnp.sum(jnp.where(lanes == rows, ref[...], 0.0), axis=1, keepdims=True)

    def layer(src, row0, parts, weights, bias_ref, emit):
        k = parts * 384
        bias = column(bias_ref)
        for n in range(6):
            acc = None
            for da in range(3):
                part = jnp.dot(weights[:, da * k:(da + 1) * k],
                               src[row0:row0 + k, (2 * n + da) * 128:(2 * n + da + 2) * 128],
                               preferred_element_type=f32)
                acc = part if acc is None else acc + part
            acc = jnp.maximum(acc + bias, 0.0)
            emit(2 * n, acc[:, :128])
            emit(2 * n + 1, acc[:, 128:])

    copies[1].wait()
    expand(wfb, z_first, 1, False)
    copies[0].wait()
    relayout(fbuf, b_feat, 0)
    layer(b_feat, 0, 1, z_first, bf_ref,
          lambda a, v: put(b_top, 384, (a + 1) * 128, v))
    copies[2].wait()
    expand(wsb, z_second, 1, True)
    layer(b_top, 384, 1, z_second, bs_ref,
          lambda a, v: put(b_mid, 0, (a + 1) * 128, v))
    copies[3].wait()
    relayout(dbuf, b_mid, 384)
    copies[4].wait()
    expand(wtb, z_third, 2, True)
    layer(b_mid, 0, 2, z_third, bt_ref,
          lambda a, v: put(b_top, 0, (a + 1) * 128, v))
    copies[5].wait()
    expand(wob, z_fourth, 2, True)

    z_head[...] = jnp.zeros((16, 128), f32)
    head = hw_ref[...].astype(f32)
    for z in range(4):
        z_head[z * 3:z * 3 + 3, z * 32:z * 32 + 28] = head
    hweight = z_head[...].astype(bf16)
    hrow = lax.broadcasted_iota(jnp.int32, (16, 128), 0)
    hlane = lax.broadcasted_iota(jnp.int32, (16, 128), 1)
    kind = lax.rem(hrow, 3)
    hbias = jnp.where(kind == 0, hb_ref[0], jnp.where(kind == 1, hb_ref[1], hb_ref[2]))
    section = hrow // 3
    depth = jnp.where((section == 0) | (section == 3), bump(0, 4), bump(1, 4))
    wave = jnp.sin((hlane.astype(f32) + 0.5) * (math.pi / 128))
    window = depth * (wave * wave)
    out_ref[...] = jnp.zeros(out_ref.shape, f32)

    def finish(a, v):
        logits = jnp.dot(hweight, v.astype(bf16), preferred_element_type=f32) + hbias
        value = jax.nn.sigmoid(logits) * (window * bump(a, 12))
        out_ref[pl.ds(3 + a, 12, stride=ROWS), :] = value[:12]

    layer(b_top, 0, 2, z_fourth, bo_ref, finish)


def conv_call(index, features, deep, wf, bfi, ws, bs, wt, bt, wo, bo, hw, hb):
    hbm = pl.BlockSpec(memory_space=pl.ANY)
    vmem = pl.BlockSpec(memory_space=pltpu.VMEM)
    smem = pl.BlockSpec(memory_space=pltpu.SMEM)
    V = pltpu.VMEM
    return pl.pallas_call(
        functools.partial(conv_kernel, index),
        out_shape=jax.ShapeDtypeStruct((12 * ROWS, 128), f32),
        in_specs=[hbm] * 6 + [vmem] * 5 + [smem],
        out_specs=vmem,
        scratch_shapes=[
            V((28, 4, 12, 128), bf16), V((28, 4, 12, 128), bf16),
            V((9, 28, 28), bf16), V((27, 28, 28), bf16), V((27, 28, 56), bf16), V((27, 28, 56), bf16),
            V((2048, 128), f32),
            V((384, 1792), bf16), V((768, 1792), bf16), V((768, 1792), bf16),
            V((128, 1152), bf16), V((128, 1152), bf16), V((128, 2304), bf16), V((128, 2304), bf16),
            V((16, 128), f32),
            pltpu.SemaphoreType.DMA((6,)),
        ],
        compiler_params=pltpu.CompilerParams(vmem_limit_bytes=48 << 20),
    )(features, deep, wf, ws, wt, wo, bfi.reshape(1, 28), bs.reshape(1, 28), bt.reshape(1, 28),
      bo.reshape(1, 28), hw, hb)


MESH = pl.DeviceIdType.MESH


def exchange_kernel(first_ref, offset_ref, planes, out_ref,
                    send_a, recv_a, send_b, recv_b, sa_sem, ra_sem, sb_sem, rb_sem):
    seg = lax.axis_index("segment")
    patch = lax.axis_index("patch")
    group = patch // 4
    turn = patch % 4
    mine = turn * 4 + seg

    def near(j):
        return {"segment": j % 4, "patch": group * 4 + j // 4}

    def far(g):
        return {"segment": seg, "patch": g * 4 + turn}

    barrier = pltpu.get_barrier_semaphore()
    for d in range(1, 16):
        pl.semaphore_signal(barrier, inc=1, device_id=near((mine + d) % 16), device_id_type=MESH)
    for d in range(1, 8):
        pl.semaphore_signal(barrier, inc=1, device_id=far((group + d) % 8), device_id_type=MESH)

    own = patch * 4 + seg
    first = first_ref[own]
    shift = 3 - offset_ref[own]

    def piece(j):
        block = (j // 4 - first + 256) % 4
        start = shift + 4 * block
        return [planes[pl.ds((j % 4 * 3 + kind) * ROWS + start, 4), :] for kind in range(3)]

    pl.semaphore_wait(barrier, 22)
    stage_a = []
    for d in range(1, 16):
        j = (mine + d) % 16
        for kind, value in enumerate(piece(j)):
            send_a[16 * d + 4 * kind:16 * d + 4 * kind + 4, :] = value
        copy = pltpu.make_async_remote_copy(
            src_ref=send_a.at[pl.ds(16 * d, 16)],
            dst_ref=recv_a.at[pl.ds(pl.multiple_of(16 * mine, 16), 16)],
            send_sem=sa_sem.at[d], recv_sem=ra_sem.at[mine],
            device_id=near(j), device_id_type=MESH)
        copy.start()
        stage_a.append(copy)
    for kind, value in enumerate(piece(mine)):
        recv_a[pl.ds(16 * mine + 4 * kind, 4), :] = value

    spot = lax.broadcasted_iota(jnp.int32, (64, 16), 1)
    rank = lax.broadcasted_iota(jnp.int32, (64, 16), 0)
    slot = jnp.zeros((64, 16), jnp.int32)
    for j in range(16):
        begin = first_ref[group * 16 + j]
        block = begin + (turn - begin + 256) % 4
        slot = jnp.where(spot == j, block // 4, slot)
    hot = (slot == (rank % 8) * 8 + rank // 8).astype(f32).astype(bf16)
    hot = jnp.concatenate([hot, hot, hot], axis=1)

    for d in range(1, 16):
        j = (mine + 16 - d) % 16
        pltpu.make_async_remote_copy(
            src_ref=send_a.at[pl.ds(16 * d, 16)],
            dst_ref=recv_a.at[pl.ds(pl.multiple_of(16 * j, 16), 16)],
            send_sem=sa_sem.at[d], recv_sem=ra_sem.at[j],
            device_id=near(j), device_id_type=MESH).wait_recv()

    columns = []
    for r in range(12):
        x = recv_a[pl.ds(r, 16, stride=16), :]
        high = x.astype(bf16)
        rest = x - high.astype(f32)
        mid = rest.astype(bf16)
        low = (rest - mid.astype(f32)).astype(bf16)
        columns.append(jnp.dot(hot, jnp.concatenate([high, mid, low], axis=0), preferred_element_type=f32))
    for r in range(12):
        v = columns[r]
        v = (v * v).reshape(8, 8, 128).astype(bf16)
        send_b[:, :, r * 128:(r + 1) * 128] = v

    stage_b = []
    for d in range(1, 8):
        g = (group + d) % 8
        copy = pltpu.make_async_remote_copy(
            src_ref=send_b.at[g], dst_ref=recv_b.at[d],
            send_sem=sb_sem.at[d], recv_sem=rb_sem.at[d],
            device_id=far(g), device_id_type=MESH)
        copy.start()
        stage_b.append(copy)
    total = jnp.sqrt(send_b[group].astype(f32))
    for copy in stage_b:
        copy.wait_recv()
    for d in range(1, 8):
        total = total + jnp.sqrt(recv_b[d].astype(f32))
    for r in range(12):
        out_ref[:, r, :] = total[:, r * 128:(r + 1) * 128]
    for copy in stage_a + stage_b:
        copy.wait_send()


def exchange_call(planes, first, offset):
    vmem = pl.BlockSpec(memory_space=pltpu.VMEM)
    smem = pl.BlockSpec(memory_space=pltpu.SMEM)
    V = pltpu.VMEM
    dma = pltpu.SemaphoreType.DMA
    return pl.pallas_call(
        exchange_kernel,
        out_shape=jax.ShapeDtypeStruct((8, 12, 128), f32),
        in_specs=[smem, smem, vmem],
        out_specs=vmem,
        scratch_shapes=[
            V((256, 128), f32), V((256, 128), f32),
            V((8, 8, 1536), bf16), V((8, 8, 1536), bf16),
            dma((16,)), dma((16,)), dma((8,)), dma((8,)),
        ],
        compiler_params=pltpu.CompilerParams(collective_id=0, has_side_effects=True),
    )(first, offset, planes)


def per_device(features, deep_path, weight_first, bias_first, weight_second, bias_second,
               weight_third, bias_third, weight_fourth, bias_fourth, head_weight, head_bias,
               block_first, block_offset):
    planes = conv_call(lambda: lax.axis_index("segment"), features, deep_path,
                       weight_first, bias_first, weight_second, bias_second,
                       weight_third, bias_third, weight_fourth, bias_fourth, head_weight, head_bias)
    blended = exchange_call(planes, block_first, block_offset)
    return blended.reshape(8, 1, 3, 1, 4, 128)


def solution(mesh):
    placed = (P("patch"), P("patch")) + (P(),) * 12
    return jax.shard_map(
        per_device,
        mesh=mesh,
        in_specs=placed,
        out_specs=P(None, "patch", None, "segment", None, None),
        check_vma=False,
    )
```

```python
import math

import jax
import jax.numpy as jnp
from jax import lax
from jax.experimental import pallas as pl
from jax.experimental.pallas import tpu as pltpu
from jax.sharding import PartitionSpec as P

bf16 = jnp.bfloat16
f32 = jnp.float32
MESH = pl.DeviceIdType.MESH
ROWS = 24


def bump(n, length):
    return math.sin(math.pi * (n + 0.5) / length) ** 2


def copies_in(s, hbm, buffers, sems):
    sources = [ref.at[s] if i < 2 else ref for i, ref in enumerate(hbm)]
    copies = [pltpu.make_async_copy(src, dst, sems.at[i])
              for i, (src, dst) in enumerate(zip(sources, buffers))]
    for i in (2, 0, 6, 3, 7, 1, 4, 8, 5, 9, 10):
        copies[i].start()
    return copies


def convolve(copies, buffers, hb_ref, planes, plane, b_feat, b_mid, b_top,
             z_first, z_second, z_third, z_fourth, z_head):
    fbuf, dbuf, wfb, wsb, wtb, wob, bf_ref, bs_ref, bt_ref, bo_ref, hw_ref = buffers

    for buf, parts in ((b_feat, 1), (b_mid, 2), (b_top, 2)):
        for side in (0, 13 * 128):
            buf[:, side:side + 128] = jnp.zeros((parts * 384, 128), bf16)
    plane[1344:1536, :] = jnp.zeros((192, 128), f32)
    planes[...] = jnp.zeros(planes.shape, f32)
    lane = lax.broadcasted_iota(jnp.int32, (128, 128), 1)

    def put(buf, row0, col0, v):
        left = jnp.where(lane > 0, pltpu.roll(v, 1, 1), 0.0)
        right = jnp.where(lane < 127, pltpu.roll(v, 127, 1), 0.0)
        buf[row0:row0 + 128, col0:col0 + 128] = left.astype(bf16)
        buf[row0 + 128:row0 + 256, col0:col0 + 128] = v.astype(bf16)
        buf[row0 + 256:row0 + 384, col0:col0 + 128] = right.astype(bf16)

    def relayout(src, buf, row0):
        plane[:1344, :] = src[...].astype(f32)
        for a in range(12):
            cell = [plane[pl.ds(4 * a + z, 32, stride=48), :] for z in range(4)]
            put(buf, row0, (a + 1) * 128, jnp.concatenate(cell, axis=0))

    def expand(w, dst, parts, full):
        dst[...] = jnp.zeros(dst.shape, bf16)
        for t in range(9):
            da, dy = t // 3, t % 3
            for part in range(parts):
                base = ((da * parts + part) * 3 + dy) * 128
                for zo in range(4):
                    for zi in range(4):
                        if abs(zi - zo) > (1 if full else 0):
                            continue
                        tap = 9 * (zi - zo + 1) + t if full else t
                        dst[zo * 32:zo * 32 + 28, base + zi * 32:base + zi * 32 + 28] = (
                            w[tap, :, part * 28:part * 28 + 28])

    def column(ref):
        lanes = lax.broadcasted_iota(jnp.int32, (128, 28), 1)
        rows = lax.rem(lax.broadcasted_iota(jnp.int32, (128, 28), 0), 32)
        return jnp.sum(jnp.where(lanes == rows, ref[...], 0.0), axis=1, keepdims=True)

    def layer(src, row0, parts, weights, bias_ref, emit):
        k = parts * 384
        bias = column(bias_ref)
        for n in range(6):
            acc = None
            for da in range(3):
                part = jnp.dot(weights[:, da * k:(da + 1) * k],
                               src[row0:row0 + k, (2 * n + da) * 128:(2 * n + da + 2) * 128],
                               preferred_element_type=f32)
                acc = part if acc is None else acc + part
            acc = jnp.maximum(acc + bias, 0.0)
            emit(2 * n, acc[:, :128])
            emit(2 * n + 1, acc[:, 128:])

    copies[2].wait()
    expand(wfb, z_first, 1, False)
    copies[0].wait()
    relayout(fbuf, b_feat, 0)
    copies[6].wait()
    layer(b_feat, 0, 1, z_first, bf_ref, lambda a, v: put(b_top, 384, (a + 1) * 128, v))
    copies[3].wait()
    expand(wsb, z_second, 1, True)
    copies[7].wait()
    layer(b_top, 384, 1, z_second, bs_ref, lambda a, v: put(b_mid, 0, (a + 1) * 128, v))
    copies[1].wait()
    relayout(dbuf, b_mid, 384)
    copies[4].wait()
    expand(wtb, z_third, 2, True)
    copies[8].wait()
    layer(b_mid, 0, 2, z_third, bt_ref, lambda a, v: put(b_top, 0, (a + 1) * 128, v))
    copies[5].wait()
    expand(wob, z_fourth, 2, True)
    copies[9].wait()
    copies[10].wait()

    z_head[...] = jnp.zeros((16, 128), f32)
    head = hw_ref[...].astype(f32)
    for z in range(4):
        z_head[z * 3:z * 3 + 3, z * 32:z * 32 + 28] = head
    hweight = z_head[...].astype(bf16)
    hrow = lax.broadcasted_iota(jnp.int32, (16, 128), 0)
    hlane = lax.broadcasted_iota(jnp.int32, (16, 128), 1)
    kind = lax.rem(hrow, 3)
    hbias = jnp.where(kind == 0, hb_ref[0], jnp.where(kind == 1, hb_ref[1], hb_ref[2]))
    depth = jnp.where((hrow < 3) | (hrow >= 9), bump(0, 4), bump(1, 4))
    wave = jnp.sin((hlane.astype(f32) + 0.5) * (math.pi / 128))
    window = depth * (wave * wave)

    def finish(a, v):
        logits = jnp.dot(hweight, v.astype(bf16), preferred_element_type=f32) + hbias
        value = jax.nn.sigmoid(logits) * (window * bump(a, 12))
        planes[pl.ds(3 + a, 12, stride=ROWS), :] = value[:12]

    layer(b_top, 0, 2, z_fourth, bo_ref, finish)


def kernel(feat, deep, wf, ws, wt, wo, bf_, bs, bt, bo, hw, hb_ref, first_ref, offset_ref, out_ref,
           fbuf, dbuf, wfb, wsb, wtb, wob, bfb, bsb, btb, bob, hwb,
           planes, plane, b_feat, b_mid, b_top, z_first, z_second, z_third, z_fourth, z_head,
           send_a, recv_a, send_b, recv_b, in_sem, sa_sem, ra_sem, sb_sem, rb_sem):
    seg = lax.axis_index("segment")
    patch = lax.axis_index("patch")
    group = patch // 4
    turn = patch % 4
    mine = turn * 4 + seg

    buffers = (fbuf, dbuf, wfb, wsb, wtb, wob, bfb, bsb, btb, bob, hwb)
    copies = copies_in(seg, (feat, deep, wf, ws, wt, wo, bf_, bs, bt, bo, hw), buffers, in_sem)

    def near(j):
        return {"segment": j % 4, "patch": group * 4 + j // 4}

    def far(g):
        return {"segment": seg, "patch": g * 4 + turn}

    barrier = pltpu.get_barrier_semaphore()
    for d in range(1, 16):
        pl.semaphore_signal(barrier, inc=1, device_id=near((mine + d) % 16), device_id_type=MESH)
    for d in range(1, 8):
        pl.semaphore_signal(barrier, inc=1, device_id=far((group + d) % 8), device_id_type=MESH)

    convolve(copies, buffers, hb_ref, planes, plane, b_feat, b_mid, b_top,
             z_first, z_second, z_third, z_fourth, z_head)

    own = patch * 4 + seg
    first = first_ref[own]
    shift = 3 - offset_ref[own]

    def piece(j):
        start = shift + 4 * ((j // 4 - first + 256) % 4)
        return [planes[pl.ds((j % 4 * 3 + kind) * ROWS + start, 4), :] for kind in range(3)]

    pl.semaphore_wait(barrier, 22)
    stage_a = []
    for d in range(1, 16):
        j = (mine + d) % 16
        for kind, value in enumerate(piece(j)):
            send_a[16 * d + 4 * kind:16 * d + 4 * kind + 4, :] = value
        copy = pltpu.make_async_remote_copy(
            src_ref=send_a.at[pl.ds(16 * d, 16)],
            dst_ref=recv_a.at[pl.ds(pl.multiple_of(16 * mine, 16), 16)],
            send_sem=sa_sem.at[d], recv_sem=ra_sem.at[mine],
            device_id=near(j), device_id_type=MESH)
        copy.start()
        stage_a.append(copy)
    for kind, value in enumerate(piece(mine)):
        recv_a[pl.ds(16 * mine + 4 * kind, 4), :] = value

    spot = lax.broadcasted_iota(jnp.int32, (64, 16), 1)
    rank = lax.broadcasted_iota(jnp.int32, (64, 16), 0)
    slot = jnp.zeros((64, 16), jnp.int32)
    for j in range(16):
        begin = first_ref[group * 16 + j]
        block = begin + (turn - begin + 256) % 4
        slot = jnp.where(spot == j, block // 4, slot)
    hot = (slot == (rank % 8) * 8 + rank // 8).astype(f32).astype(bf16)
    hot = jnp.concatenate([hot, hot, hot], axis=1)

    for d in range(1, 16):
        j = (mine + 16 - d) % 16
        pltpu.make_async_remote_copy(
            src_ref=send_a.at[pl.ds(16 * d, 16)],
            dst_ref=recv_a.at[pl.ds(pl.multiple_of(16 * j, 16), 16)],
            send_sem=sa_sem.at[d], recv_sem=ra_sem.at[j],
            device_id=near(j), device_id_type=MESH).wait_recv()

    sums = []
    for r in range(12):
        x = recv_a[pl.ds(r, 16, stride=16), :]
        high = x.astype(bf16)
        rest = x - high.astype(f32)
        mid = rest.astype(bf16)
        low = (rest - mid.astype(f32)).astype(bf16)
        sums.append(jnp.dot(hot, jnp.concatenate([high, mid, low], axis=0), preferred_element_type=f32))
    for r in range(12):
        send_b[:, :, r * 128:(r + 1) * 128] = (sums[r] * sums[r]).reshape(8, 8, 128).astype(bf16)

    stage_b = []
    for d in range(1, 8):
        g = (group + d) % 8
        copy = pltpu.make_async_remote_copy(
            src_ref=send_b.at[g], dst_ref=recv_b.at[d],
            send_sem=sb_sem.at[d], recv_sem=rb_sem.at[d],
            device_id=far(g), device_id_type=MESH)
        copy.start()
        stage_b.append(copy)
    total = jnp.sqrt(send_b[group].astype(f32))
    for copy in stage_b:
        copy.wait_recv()
    for d in range(1, 8):
        total = total + jnp.sqrt(recv_b[d].astype(f32))
    for r in range(12):
        out_ref[pl.ds(r, 8, stride=12), :] = total[:, r * 128:(r + 1) * 128]
    for copy in stage_a + stage_b:
        copy.wait_send()


def per_device(features, deep_path, weight_first, bias_first, weight_second, bias_second,
               weight_third, bias_third, weight_fourth, bias_fourth, head_weight, head_bias,
               block_first, block_offset):
    def rows(x):
        return x.transpose(0, 1, 3, 2, 4).reshape(4, 1344, 128)

    hbm = pl.BlockSpec(memory_space=pltpu.HBM)
    vmem = pl.BlockSpec(memory_space=pltpu.VMEM)
    smem = pl.BlockSpec(memory_space=pltpu.SMEM)
    V = pltpu.VMEM
    dma = pltpu.SemaphoreType.DMA
    blended = pl.pallas_call(
        kernel,
        out_shape=jax.ShapeDtypeStruct((96, 128), f32),
        in_specs=[hbm] * 11 + [smem] * 3,
        out_specs=vmem,
        scratch_shapes=[
            V((1344, 128), bf16), V((1344, 128), bf16),
            V((9, 28, 28), bf16), V((27, 28, 28), bf16), V((27, 28, 56), bf16), V((27, 28, 56), bf16),
            V((1, 28), f32), V((1, 28), f32), V((1, 28), f32), V((1, 28), f32), V((3, 28), bf16),
            V((12 * ROWS, 128), f32), V((1536, 128), f32),
            V((384, 1792), bf16), V((768, 1792), bf16), V((768, 1792), bf16),
            V((128, 1152), bf16), V((128, 1152), bf16), V((128, 2304), bf16), V((128, 2304), bf16),
            V((16, 128), f32),
            V((256, 128), f32), V((256, 128), f32), V((8, 8, 1536), bf16), V((8, 8, 1536), bf16),
            dma((11,)), dma((16,)), dma((16,)), dma((8,)), dma((8,)),
        ],
        compiler_params=pltpu.CompilerParams(
            collective_id=0, has_side_effects=True, vmem_limit_bytes=60 << 20),
    )(rows(features), rows(deep_path), weight_first, weight_second, weight_third, weight_fourth,
      bias_first.reshape(1, 28), bias_second.reshape(1, 28), bias_third.reshape(1, 28),
      bias_fourth.reshape(1, 28), head_weight, head_bias, block_first, block_offset)
    return blended.reshape(8, 1, 3, 1, 4, 128)


def solution(mesh):
    placed = (P("patch"), P("patch")) + (P(),) * 12
    return jax.shard_map(
        per_device,
        mesh=mesh,
        in_specs=placed,
        out_specs=P(None, "patch", None, "segment", None, None),
        check_vma=False,
    )
```

```python
import math

import jax
import jax.numpy as jnp
from jax import lax
from jax.experimental import pallas as pl
from jax.experimental.pallas import tpu as pltpu
from jax.sharding import PartitionSpec as P

bf16 = jnp.bfloat16
f32 = jnp.float32
MESH = pl.DeviceIdType.MESH
ROWS = 24


def bump(n, length):
    return math.sin(math.pi * (n + 0.5) / length) ** 2


def copies_in(s, hbm, buffers, sems):
    sources = [ref.at[s] if i < 2 else ref for i, ref in enumerate(hbm)]
    copies = [pltpu.make_async_copy(src, dst, sems.at[i])
              for i, (src, dst) in enumerate(zip(sources, buffers))]
    for i in (2, 0, 6, 3, 7, 1, 4, 8, 5, 9, 10):
        copies[i].start()
    return copies


def convolve(copies, buffers, hb_ref, planes, plane, b_feat, b_mid, b_top,
             z_first, z_second, z_third, z_fourth, z_head):
    fbuf, dbuf, wfb, wsb, wtb, wob, bf_ref, bs_ref, bt_ref, bo_ref, hw_ref = buffers

    plane[1344:1536, :] = jnp.zeros((192, 128), f32)
    planes[...] = jnp.zeros(planes.shape, f32)
    lane = lax.broadcasted_iota(jnp.int32, (128, 128), 1)

    def put(buf, row0, col0, v):
        v = v.astype(bf16)
        zero = jnp.zeros((128, 128), bf16)
        buf[row0:row0 + 128, col0:col0 + 128] = jnp.where(lane > 0, pltpu.roll(v, 1, 1), zero)
        buf[row0 + 128:row0 + 256, col0:col0 + 128] = v
        buf[row0 + 256:row0 + 384, col0:col0 + 128] = jnp.where(lane < 127, pltpu.roll(v, 127, 1), zero)

    def relayout(src, buf, row0):
        for c in range(0, 1344, 336):
            plane[c:c + 336, :] = src[c:c + 336, :].astype(f32)
            yield
        for a in range(12):
            cell = [plane[pl.ds(4 * a + z, 32, stride=48), :] for z in range(4)]
            put(buf, row0, a * 128, jnp.concatenate(cell, axis=0))
            yield

    def expand(w, dst, parts, full):
        dst[...] = jnp.zeros(dst.shape, bf16)
        for t in range(9):
            da, dy = t // 3, t % 3
            for part in range(parts):
                base = (part * 3 + dy) * 128
                for zo in range(4):
                    for zi in range(4):
                        if abs(zi - zo) > (1 if full else 0):
                            continue
                        tap = 9 * (zi - zo + 1) + t if full else t
                        dst[da * 128 + zo * 32:da * 128 + zo * 32 + 28, base + zi * 32:base + zi * 32 + 28] = (
                            w[tap, :, part * 28:part * 28 + 28])
                yield

    def column(ref):
        lanes = lax.broadcasted_iota(jnp.int32, (128, 28), 1)
        rows = lax.rem(lax.broadcasted_iota(jnp.int32, (128, 28), 0), 32)
        return jnp.sum(jnp.where(lanes == rows, ref[...], 0.0), axis=1, keepdims=True)

    def layer(src, row0, parts, weights, bias_ref, emit, beside=()):
        k = parts * 384
        bias = column(bias_ref)
        sums = {}
        for n in range(6):
            p = jnp.dot(weights[...], src[row0:row0 + k, n * 256:(n + 1) * 256],
                        preferred_element_type=f32)
            for task, count in beside:
                for _ in range(count):
                    next(task, None)
            for b in (2 * n, 2 * n + 1):
                for da in (2, 1, 0):
                    a = b + 1 - da
                    if 0 <= a < 12:
                        term = p[da * 128:(da + 1) * 128, (b - 2 * n) * 128:(b - 2 * n + 1) * 128]
                        sums[a] = sums[a] + term if a in sums else term
            for a in (2 * n - 1, 2 * n) + ((11,) if n == 5 else ()):
                if a >= 0:
                    emit(a, jnp.maximum(sums.pop(a) + bias, 0.0))

    def run(task):
        for _ in task:
            pass

    copies[2].wait()
    run(expand(wfb, z_first, 1, False))
    copies[0].wait()
    run(relayout(fbuf, b_feat, 0))
    for i in (6, 3, 7, 1):
        copies[i].wait()
    second = expand(wsb, z_second, 1, True)
    deeper = relayout(dbuf, b_mid, 384)
    layer(b_feat, 0, 1, z_first, bf_ref, lambda a, v: put(b_top, 384, a * 128, v), [(second, 2), (deeper, 2)])
    run(second)
    for i in (4, 8, 5):
        copies[i].wait()
    third = expand(wtb, z_third, 2, True)
    fourth = expand(wob, z_fourth, 2, True)
    layer(b_top, 384, 1, z_second, bs_ref, lambda a, v: put(b_mid, 0, a * 128, v), [(deeper, 3), (third, 3)])
    run(deeper)
    run(third)
    layer(b_mid, 0, 2, z_third, bt_ref, lambda a, v: put(b_top, 0, a * 128, v), [(fourth, 3)])
    run(fourth)
    copies[9].wait()
    copies[10].wait()

    z_head[...] = jnp.zeros((16, 128), f32)
    head = hw_ref[...].astype(f32)
    for z in range(4):
        z_head[z * 3:z * 3 + 3, z * 32:z * 32 + 28] = head
    hweight = z_head[...].astype(bf16)
    hrow = lax.broadcasted_iota(jnp.int32, (16, 128), 0)
    hlane = lax.broadcasted_iota(jnp.int32, (16, 128), 1)
    kind = lax.rem(hrow, 3)
    hbias = jnp.where(kind == 0, hb_ref[0], jnp.where(kind == 1, hb_ref[1], hb_ref[2]))
    depth = jnp.where((hrow < 3) | (hrow >= 9), bump(0, 4), bump(1, 4))
    wave = jnp.sin((hlane.astype(f32) + 0.5) * (math.pi / 128))
    window = depth * (wave * wave)

    def keep(a, v):
        b_feat[0:128, a * 128:(a + 1) * 128] = v.astype(bf16)

    layer(b_top, 0, 2, z_fourth, bo_ref, keep)
    logits = jnp.dot(hweight, b_feat[0:128, :], preferred_element_type=f32)
    for a in range(12):
        value = jax.nn.sigmoid(logits[:, a * 128:(a + 1) * 128] + hbias) * (window * bump(a, 12))
        planes[pl.ds(3 + a, 12, stride=ROWS), :] = value[:12]


def kernel(feat, deep, wf, ws, wt, wo, bf_, bs, bt, bo, hw, hb_ref, first_ref, offset_ref, out_ref,
           fbuf, dbuf, wfb, wsb, wtb, wob, bfb, bsb, btb, bob, hwb,
           planes, plane, b_feat, b_mid, b_top, z_first, z_second, z_third, z_fourth, z_head,
           send_a, recv_a, send_b, recv_b, in_sem, sa_sem, ra_sem, sb_sem, rb_sem):
    seg = lax.axis_index("segment")
    patch = lax.axis_index("patch")
    group = patch // 4
    turn = patch % 4
    mine = turn * 4 + seg

    buffers = (fbuf, dbuf, wfb, wsb, wtb, wob, bfb, bsb, btb, bob, hwb)
    copies = copies_in(seg, (feat, deep, wf, ws, wt, wo, bf_, bs, bt, bo, hw), buffers, in_sem)

    def near(j):
        return {"segment": j % 4, "patch": group * 4 + j // 4}

    def far(g):
        return {"segment": seg, "patch": g * 4 + turn}

    barrier = pltpu.get_barrier_semaphore()
    for d in range(1, 16):
        pl.semaphore_signal(barrier, inc=1, device_id=near((mine + d) % 16), device_id_type=MESH)
    for d in range(1, 8):
        pl.semaphore_signal(barrier, inc=1, device_id=far((group + d) % 8), device_id_type=MESH)

    convolve(copies, buffers, hb_ref, planes, plane, b_feat, b_mid, b_top,
             z_first, z_second, z_third, z_fourth, z_head)

    own = patch * 4 + seg
    first = first_ref[own]
    shift = 3 - offset_ref[own]

    def piece(j):
        start = shift + 4 * ((j // 4 - first + 256) % 4)
        return [planes[pl.ds((j % 4 * 3 + kind) * ROWS + start, 4), :] for kind in range(3)]

    pl.semaphore_wait(barrier, 22)
    stage_a = []
    for d in range(1, 16):
        j = (mine + d) % 16
        for kind, value in enumerate(piece(j)):
            send_a[16 * d + 4 * kind:16 * d + 4 * kind + 4, :] = value
        copy = pltpu.make_async_remote_copy(
            src_ref=send_a.at[pl.ds(16 * d, 16)],
            dst_ref=recv_a.at[pl.ds(pl.multiple_of(16 * mine, 16), 16)],
            send_sem=sa_sem.at[d], recv_sem=ra_sem.at[mine],
            device_id=near(j), device_id_type=MESH)
        copy.start()
        stage_a.append(copy)
    for kind, value in enumerate(piece(mine)):
        recv_a[pl.ds(16 * mine + 4 * kind, 4), :] = value

    spot = lax.broadcasted_iota(jnp.int32, (64, 16), 1)
    rank = lax.broadcasted_iota(jnp.int32, (64, 16), 0)
    slot = jnp.zeros((64, 16), jnp.int32)
    for j in range(16):
        begin = first_ref[group * 16 + j]
        block = begin + (turn - begin + 256) % 4
        slot = jnp.where(spot == j, block // 4, slot)
    hot = (slot == (rank % 8) * 8 + rank // 8).astype(f32).astype(bf16)
    hot = jnp.concatenate([hot, hot, hot], axis=1)

    for d in range(1, 16):
        j = (mine + 16 - d) % 16
        pltpu.make_async_remote_copy(
            src_ref=send_a.at[pl.ds(16 * d, 16)],
            dst_ref=recv_a.at[pl.ds(pl.multiple_of(16 * j, 16), 16)],
            send_sem=sa_sem.at[d], recv_sem=ra_sem.at[j],
            device_id=near(j), device_id_type=MESH).wait_recv()

    sums = []
    for r in range(12):
        x = recv_a[pl.ds(r, 16, stride=16), :]
        high = x.astype(bf16)
        rest = x - high.astype(f32)
        mid = rest.astype(bf16)
        low = (rest - mid.astype(f32)).astype(bf16)
        sums.append(jnp.dot(hot, jnp.concatenate([high, mid, low], axis=0), preferred_element_type=f32))
    for r in range(12):
        send_b[:, :, r * 128:(r + 1) * 128] = (sums[r] * sums[r]).reshape(8, 8, 128).astype(bf16)

    stage_b = []
    for d in range(1, 8):
        g = (group + d) % 8
        copy = pltpu.make_async_remote_copy(
            src_ref=send_b.at[g], dst_ref=recv_b.at[d],
            send_sem=sb_sem.at[d], recv_sem=rb_sem.at[d],
            device_id=far(g), device_id_type=MESH)
        copy.start()
        stage_b.append(copy)
    total = jnp.sqrt(send_b[group].astype(f32))
    for copy in stage_b:
        copy.wait_recv()
    for d in range(1, 8):
        total = total + jnp.sqrt(recv_b[d].astype(f32))
    for r in range(12):
        out_ref[pl.ds(r, 8, stride=12), :] = total[:, r * 128:(r + 1) * 128]
    for copy in stage_a + stage_b:
        copy.wait_send()


def conv_buffers():
    V = pltpu.VMEM
    return [
        V((1344, 128), bf16), V((1344, 128), bf16),
        V((9, 28, 28), bf16), V((27, 28, 28), bf16), V((27, 28, 56), bf16), V((27, 28, 56), bf16),
        V((1, 28), f32), V((1, 28), f32), V((1, 28), f32), V((1, 28), f32), V((3, 28), bf16),
    ]


def conv_scratch():
    V = pltpu.VMEM
    return [
        V((1536, 128), f32),
        V((384, 1536), bf16), V((768, 1536), bf16), V((768, 1536), bf16),
        V((384, 384), bf16), V((384, 384), bf16), V((384, 768), bf16), V((384, 768), bf16),
        V((16, 128), f32),
    ]


def per_device(features, deep_path, weight_first, bias_first, weight_second, bias_second,
               weight_third, bias_third, weight_fourth, bias_fourth, head_weight, head_bias,
               block_first, block_offset):
    def rows(x):
        return x.transpose(0, 1, 3, 2, 4).reshape(4, 1344, 128)

    hbm = pl.BlockSpec(memory_space=pltpu.HBM)
    vmem = pl.BlockSpec(memory_space=pltpu.VMEM)
    smem = pl.BlockSpec(memory_space=pltpu.SMEM)
    V = pltpu.VMEM
    dma = pltpu.SemaphoreType.DMA
    blended = pl.pallas_call(
        kernel,
        out_shape=jax.ShapeDtypeStruct((96, 128), f32),
        in_specs=[hbm] * 11 + [smem] * 3,
        out_specs=vmem,
        scratch_shapes=conv_buffers() + [V((12 * ROWS, 128), f32)] + conv_scratch() + [
            V((256, 128), f32), V((256, 128), f32), V((8, 8, 1536), bf16), V((8, 8, 1536), bf16),
            dma((11,)), dma((16,)), dma((16,)), dma((8,)), dma((8,)),
        ],
        compiler_params=pltpu.CompilerParams(
            collective_id=0, has_side_effects=True, vmem_limit_bytes=60 << 20),
    )(rows(features), rows(deep_path), weight_first, weight_second, weight_third, weight_fourth,
      bias_first.reshape(1, 28), bias_second.reshape(1, 28), bias_third.reshape(1, 28),
      bias_fourth.reshape(1, 28), head_weight, head_bias, block_first, block_offset)
    return blended.reshape(8, 1, 3, 1, 4, 128)


def solution(mesh):
    placed = (P("patch"), P("patch")) + (P(),) * 12
    return jax.shard_map(
        per_device,
        mesh=mesh,
        in_specs=placed,
        out_specs=P(None, "patch", None, "segment", None, None),
        check_vma=False,
    )
```

```python
import math

import jax
import jax.numpy as jnp
from jax import lax
from jax.experimental import pallas as pl
from jax.experimental.pallas import tpu as pltpu
from jax.sharding import PartitionSpec as P

bf16 = jnp.bfloat16
f32 = jnp.float32
MESH = pl.DeviceIdType.MESH
ROWS = 24


def bump(n, length):
    return math.sin(math.pi * (n + 0.5) / length) ** 2


def copies_in(s, hbm, buffers, sems):
    sources = [ref.at[s] if i < 2 else ref for i, ref in enumerate(hbm)]
    copies = [pltpu.make_async_copy(src, dst, sems.at[i])
              for i, (src, dst) in enumerate(zip(sources, buffers))]
    for i in (2, 0, 6, 3, 7, 1, 4, 8, 5, 9, 10):
        copies[i].start()
    return copies


def convolve(copies, buffers, hb_ref, planes, plane, b_feat, b_mid, b_top,
             z_first, z_second, z_third, z_fourth, z_head):
    fbuf, dbuf, wfb, wsb, wtb, wob, bf_ref, bs_ref, bt_ref, bo_ref, hw_ref = buffers

    plane[1344:1536, :] = jnp.zeros((192, 128), f32)
    planes[...] = jnp.zeros(planes.shape, f32)
    lane = lax.broadcasted_iota(jnp.int32, (128, 128), 1)

    def put(buf, row0, col0, v):
        v = v.astype(bf16)
        zero = jnp.zeros((128, 128), bf16)
        buf[row0:row0 + 128, col0:col0 + 128] = jnp.where(lane > 0, pltpu.roll(v, 1, 1), zero)
        buf[row0 + 128:row0 + 256, col0:col0 + 128] = v
        buf[row0 + 256:row0 + 384, col0:col0 + 128] = jnp.where(lane < 127, pltpu.roll(v, 127, 1), zero)

    def relayout(src, buf, row0):
        for c in range(0, 1344, 336):
            plane[c:c + 336, :] = src[c:c + 336, :].astype(f32)
            yield
        for a in range(12):
            cell = [plane[pl.ds(4 * a + z, 32, stride=48), :] for z in range(4)]
            put(buf, row0, a * 128, jnp.concatenate(cell, axis=0))
            yield

    def expand(w, dst, parts, full):
        dst[...] = jnp.zeros(dst.shape, bf16)
        for t in range(9):
            da, dy = t // 3, t % 3
            for part in range(parts):
                base = (part * 3 + dy) * 128
                for zo in range(4):
                    for zi in range(4):
                        if abs(zi - zo) > (1 if full else 0):
                            continue
                        tap = 9 * (zi - zo + 1) + t if full else t
                        dst[da * 128 + zo * 32:da * 128 + zo * 32 + 28, base + zi * 32:base + zi * 32 + 28] = (
                            w[tap, :, part * 28:part * 28 + 28])
                yield

    def column(ref):
        lanes = lax.broadcasted_iota(jnp.int32, (128, 28), 1)
        rows = lax.rem(lax.broadcasted_iota(jnp.int32, (128, 28), 0), 32)
        return jnp.sum(jnp.where(lanes == rows, ref[...], 0.0), axis=1, keepdims=True)

    def layer(src, row0, parts, weights, bias_ref, emit, beside=()):
        k = parts * 384
        bias = column(bias_ref)
        sums = {}
        for n in range(6):
            p = jnp.dot(weights[...], src[row0:row0 + k, n * 256:(n + 1) * 256],
                        preferred_element_type=f32)
            for task, count in beside:
                for _ in range(count):
                    next(task, None)
            for b in (2 * n, 2 * n + 1):
                for da in (2, 1, 0):
                    a = b + 1 - da
                    if 0 <= a < 12:
                        term = p[da * 128:(da + 1) * 128, (b - 2 * n) * 128:(b - 2 * n + 1) * 128]
                        sums[a] = sums[a] + term if a in sums else term
            for a in (2 * n - 1, 2 * n) + ((11,) if n == 5 else ()):
                if a >= 0:
                    emit(a, jnp.maximum(sums.pop(a) + bias, 0.0))

    def run(task):
        for _ in task:
            pass

    copies[2].wait()
    run(expand(wfb, z_first, 1, False))
    copies[0].wait()
    run(relayout(fbuf, b_feat, 0))
    for i in (6, 3, 7, 1):
        copies[i].wait()
    second = expand(wsb, z_second, 1, True)
    deeper = relayout(dbuf, b_mid, 384)
    layer(b_feat, 0, 1, z_first, bf_ref, lambda a, v: put(b_top, 384, a * 128, v), [(second, 2), (deeper, 2)])
    run(second)
    for i in (4, 8, 5):
        copies[i].wait()
    third = expand(wtb, z_third, 2, True)
    fourth = expand(wob, z_fourth, 2, True)
    layer(b_top, 384, 1, z_second, bs_ref, lambda a, v: put(b_mid, 0, a * 128, v), [(deeper, 3), (third, 3)])
    run(deeper)
    run(third)
    layer(b_mid, 0, 2, z_third, bt_ref, lambda a, v: put(b_top, 0, a * 128, v), [(fourth, 3)])
    run(fourth)
    copies[9].wait()
    copies[10].wait()

    z_head[...] = jnp.zeros((16, 128), f32)
    head = hw_ref[...].astype(f32)
    for z in range(4):
        z_head[z * 3:z * 3 + 3, z * 32:z * 32 + 28] = head
    hweight = z_head[...].astype(bf16)
    hrow = lax.broadcasted_iota(jnp.int32, (16, 128), 0)
    hlane = lax.broadcasted_iota(jnp.int32, (16, 128), 1)
    kind = lax.rem(hrow, 3)
    hbias = jnp.where(kind == 0, hb_ref[0], jnp.where(kind == 1, hb_ref[1], hb_ref[2]))
    depth = jnp.where((hrow < 3) | (hrow >= 9), bump(0, 4), bump(1, 4))
    wave = jnp.sin((hlane.astype(f32) + 0.5) * (math.pi / 128))
    window = depth * (wave * wave)

    def keep(a, v):
        b_feat[0:128, a * 128:(a + 1) * 128] = v.astype(bf16)

    layer(b_top, 0, 2, z_fourth, bo_ref, keep)
    logits = jnp.dot(hweight, b_feat[0:128, :], preferred_element_type=f32)
    for a in range(12):
        value = jax.nn.sigmoid(logits[:, a * 128:(a + 1) * 128] + hbias) * (window * bump(a, 12))
        planes[pl.ds(3 + a, 12, stride=ROWS), :] = value[:12]


def kernel(feat, deep, wf, ws, wt, wo, bf_, bs, bt, bo, hw, hb_ref, first_ref, offset_ref, out_ref,
           fbuf, dbuf, wfb, wsb, wtb, wob, bfb, bsb, btb, bob, hwb,
           planes, plane, b_feat, b_mid, b_top, z_first, z_second, z_third, z_fourth, z_head,
           hot_ref, send_a, recv_a, pieces, send_b, recv_b, in_sem, sa_sem, ra_sem, sb_sem, rb_sem):
    seg = lax.axis_index("segment")
    patch = lax.axis_index("patch")
    half = patch // 16
    line = patch // 4 % 4
    turn = patch % 4
    mine = turn * 4 + seg

    buffers = (fbuf, dbuf, wfb, wsb, wtb, wob, bfb, bsb, btb, bob, hwb)
    copies = copies_in(seg, (feat, deep, wf, ws, wt, wo, bf_, bs, bt, bo, hw), buffers, in_sem)

    def near(h, j):
        return {"segment": j % 4, "patch": (h * 4 + line) * 4 + j // 4}

    def along(y):
        return {"segment": seg, "patch": (half * 4 + y) * 4 + turn}

    others = [(h, d) for h in (1, 0) for d in range(16) if h or d]
    barrier = pltpu.get_barrier_semaphore()
    for h, d in others:
        pl.semaphore_signal(barrier, inc=1, device_id=near((half + h) % 2, (mine + d) % 16),
                            device_id_type=MESH)
    for d in range(1, 4):
        pl.semaphore_signal(barrier, inc=1, device_id=along((line + d) % 4), device_id_type=MESH)

    spot = lax.broadcasted_iota(jnp.int32, (32, 32), 1)
    rank = lax.broadcasted_iota(jnp.int32, (32, 32), 0)
    slot = jnp.zeros((32, 32), jnp.int32)
    for j in range(32):
        begin = first_ref[(j // 16 * 4 + line) * 16 + j % 16]
        block = begin + (turn - begin + 256) % 4
        slot = jnp.where(spot == j, block // 4, slot)
    goal = (rank % 8) * 8 + half * 4 + (rank // 8 + line) % 4
    hot_ref[...] = (slot == goal).astype(f32)

    convolve(copies, buffers, hb_ref, planes, plane, b_feat, b_mid, b_top,
             z_first, z_second, z_third, z_fourth, z_head)

    own = patch * 4 + seg
    first = first_ref[own]
    shift = 3 - offset_ref[own]

    def piece(j):
        start = shift + 4 * ((j // 4 - first + 256) % 4)
        value = jnp.concatenate(
            [planes[pl.ds((j % 4 * 3 + kind) * ROWS + start, 4), :] for kind in range(3)], axis=0)
        return (value * value).astype(bf16)

    for d in range(16):
        send_a[d] = piece((mine + d) % 16)
    pl.semaphore_wait(barrier, 34)
    stage_a = []
    for n, (h, d) in enumerate(others):
        copy = pltpu.make_async_remote_copy(
            src_ref=send_a.at[d], dst_ref=recv_a.at[half * 16 + mine],
            send_sem=sa_sem.at[n], recv_sem=ra_sem.at[half * 16 + mine],
            device_id=near((half + h) % 2, (mine + d) % 16), device_id_type=MESH)
        copy.start()
        stage_a.append(copy)
    recv_a[half * 16 + mine] = send_a[0]
    for n, (h, d) in enumerate(others):
        j = (half + h) % 2 * 16 + (mine + 16 - d) % 16
        pltpu.make_async_remote_copy(
            src_ref=send_a.at[d], dst_ref=recv_a.at[j],
            send_sem=sa_sem.at[n], recv_sem=ra_sem.at[j],
            device_id=near((half + h) % 2, (mine + 16 - d) % 16), device_id_type=MESH).wait_recv()

    for j in range(32):
        pieces[16 * j:16 * j + 12, :] = jnp.sqrt(recv_a[j].astype(f32))
    hot = hot_ref[...].astype(bf16)
    hot = jnp.concatenate([hot, hot], axis=1)
    for r in range(12):
        x = pieces[pl.ds(r, 32, stride=16), :]
        high = x.astype(bf16)
        low = (x - high.astype(f32)).astype(bf16)
        v = jnp.dot(hot, jnp.concatenate([high, low], axis=0), preferred_element_type=f32)
        v = v * v
        send_b[:, :, r * 128:(r + 1) * 128] = (v * v).reshape(4, 8, 128).astype(bf16)

    stage_b = []
    for d in (2, 1, 3):
        copy = pltpu.make_async_remote_copy(
            src_ref=send_b.at[d], dst_ref=recv_b.at[d],
            send_sem=sb_sem.at[d], recv_sem=rb_sem.at[d],
            device_id=along((line + d) % 4), device_id_type=MESH)
        copy.start()
        stage_b.append(copy)

    def decode(x):
        return jnp.sqrt(jnp.sqrt(x.astype(f32)))

    total = decode(send_b[0])
    for copy in stage_b:
        copy.wait_recv()
    for d in range(1, 4):
        total = total + decode(recv_b[d])
    for r in range(12):
        out_ref[pl.ds(r, 8, stride=12), :] = total[:, r * 128:(r + 1) * 128]
    for copy in stage_a + stage_b:
        copy.wait_send()


def conv_buffers():
    V = pltpu.VMEM
    return [
        V((1344, 128), bf16), V((1344, 128), bf16),
        V((9, 28, 28), bf16), V((27, 28, 28), bf16), V((27, 28, 56), bf16), V((27, 28, 56), bf16),
        V((1, 28), f32), V((1, 28), f32), V((1, 28), f32), V((1, 28), f32), V((3, 28), bf16),
    ]


def conv_scratch():
    V = pltpu.VMEM
    return [
        V((1536, 128), f32),
        V((384, 1536), bf16), V((768, 1536), bf16), V((768, 1536), bf16),
        V((384, 384), bf16), V((384, 384), bf16), V((384, 768), bf16), V((384, 768), bf16),
        V((16, 128), f32),
    ]


def per_device(features, deep_path, weight_first, bias_first, weight_second, bias_second,
               weight_third, bias_third, weight_fourth, bias_fourth, head_weight, head_bias,
               block_first, block_offset):
    def rows(x):
        return x.transpose(0, 1, 3, 2, 4).reshape(4, 1344, 128)

    hbm = pl.BlockSpec(memory_space=pltpu.HBM)
    vmem = pl.BlockSpec(memory_space=pltpu.VMEM)
    smem = pl.BlockSpec(memory_space=pltpu.SMEM)
    V = pltpu.VMEM
    dma = pltpu.SemaphoreType.DMA
    blended = pl.pallas_call(
        kernel,
        out_shape=V((96, 128), f32),
        in_specs=[hbm] * 11 + [smem] * 3,
        out_specs=vmem,
        scratch_shapes=conv_buffers() + [V((12 * ROWS, 128), f32)] + conv_scratch() + [
            V((32, 32), f32), V((16, 12, 128), bf16), V((32, 12, 128), bf16), V((512, 128), f32),
            V((4, 8, 1536), bf16), V((4, 8, 1536), bf16),
            dma((11,)), dma((31,)), dma((32,)), dma((4,)), dma((4,)),
        ],
        compiler_params=pltpu.CompilerParams(
            collective_id=0, has_side_effects=True, vmem_limit_bytes=60 << 20),
    )(rows(features), rows(deep_path), weight_first, weight_second, weight_third, weight_fourth,
      bias_first.reshape(1, 28), bias_second.reshape(1, 28), bias_third.reshape(1, 28),
      bias_fourth.reshape(1, 28), head_weight, head_bias, block_first, block_offset)
    return blended.reshape(8, 1, 3, 1, 4, 128)


def solution(mesh):
    placed = (P("patch"), P("patch")) + (P(),) * 12
    return jax.shard_map(
        per_device,
        mesh=mesh,
        in_specs=placed,
        out_specs=P(None, "patch", None, "segment", None, None),
        check_vma=False,
    )
```

```python
import math

import jax
import jax.numpy as jnp
from jax import lax
from jax.experimental import pallas as pl
from jax.experimental.pallas import tpu as pltpu
from jax.sharding import PartitionSpec as P

bf16 = jnp.bfloat16
f32 = jnp.float32
LOGICAL = pl.DeviceIdType.LOGICAL
ROWS = 24


def bump(n, length):
    return math.sin(math.pi * (n + 0.5) / length) ** 2


def copies_in(s, hbm, buffers, sems):
    sources = [ref.at[s] if i < 2 else ref for i, ref in enumerate(hbm)]
    copies = [pltpu.make_async_copy(src, dst, sems.at[i])
              for i, (src, dst) in enumerate(zip(sources, buffers))]
    for i in (2, 0, 6, 3, 7, 1, 4, 8, 5, 9, 10):
        copies[i].start()
    return copies


def convolve(copies, slots, buffers, hb_ref, planes, plane, b_feat, b_mid, b_top,
             z_first, z_second, z_third, z_fourth, z_head):
    fbuf, dbuf, wfb, wsb, wtb, wob, bf_ref, bs_ref, bt_ref, bo_ref, hw_ref = buffers

    plane[1344:1536, :] = jnp.zeros((192, 128), f32)
    planes[...] = jnp.zeros(planes.shape, f32)
    for dst in (z_first, z_second, z_third, z_fourth):
        dst[...] = jnp.zeros(dst.shape, bf16)
    lane = lax.broadcasted_iota(jnp.int32, (128, 128), 1)

    def put(buf, row0, col0, v):
        v = v.astype(bf16)
        zero = jnp.zeros((128, 128), bf16)
        buf[row0:row0 + 128, col0:col0 + 128] = jnp.where(lane > 0, pltpu.roll(v, 1, 1), zero)
        buf[row0 + 128:row0 + 256, col0:col0 + 128] = v
        buf[row0 + 256:row0 + 384, col0:col0 + 128] = jnp.where(lane < 127, pltpu.roll(v, 127, 1), zero)

    def relayout(src, buf, row0):
        for c in range(0, 1344, 336):
            plane[c:c + 336, :] = src[c:c + 336, :].astype(f32)
            yield
        for a in range(12):
            cell = [plane[pl.ds(4 * a + z, 32, stride=48), :] for z in range(4)]
            put(buf, row0, a * 128, jnp.concatenate(cell, axis=0))
            yield

    def expand(w, dst, parts, full):
        for t in range(9):
            da, dy = t // 3, t % 3
            for part in range(parts):
                base = (part * 3 + dy) * 128
                for zo in range(4):
                    for zi in range(4):
                        if abs(zi - zo) > (1 if full else 0):
                            continue
                        tap = 9 * (zi - zo + 1) + t if full else t
                        dst[da * 128 + zo * 32:da * 128 + zo * 32 + 28, base + zi * 32:base + zi * 32 + 28] = (
                            w[tap, :, part * 28:part * 28 + 28])
                yield

    def column(ref):
        lanes = lax.broadcasted_iota(jnp.int32, (128, 28), 1)
        rows = lax.rem(lax.broadcasted_iota(jnp.int32, (128, 28), 0), 32)
        return jnp.sum(jnp.where(lanes == rows, ref[...], 0.0), axis=1, keepdims=True)

    def layer(src, row0, parts, weights, bias_ref, emit, beside=()):
        k = parts * 384
        bias = column(bias_ref)
        sums = {}
        for n in range(6):
            p = jnp.dot(weights[...], src[row0:row0 + k, n * 256:(n + 1) * 256],
                        preferred_element_type=f32)
            for task, count in beside:
                for _ in range(count):
                    next(task, None)
            for b in (2 * n, 2 * n + 1):
                for da in (2, 1, 0):
                    a = b + 1 - da
                    if 0 <= a < 12:
                        term = p[da * 128:(da + 1) * 128, (b - 2 * n) * 128:(b - 2 * n + 1) * 128]
                        sums[a] = sums[a] + term if a in sums else term
            for a in (2 * n - 1, 2 * n) + ((11,) if n == 5 else ()):
                if a >= 0:
                    emit(a, jnp.maximum(sums.pop(a) + bias, 0.0))

    def run(task):
        for _ in task:
            pass

    copies[2].wait()
    run(expand(wfb, z_first, 1, False))
    copies[0].wait()
    run(relayout(fbuf, b_feat, 0))
    for i in (6, 3, 7, 1):
        copies[i].wait()
    second = expand(wsb, z_second, 1, True)
    deeper = relayout(dbuf, b_mid, 384)
    layer(b_feat, 0, 1, z_first, bf_ref, lambda a, v: put(b_top, 384, a * 128, v), [(second, 2), (deeper, 2)])
    run(second)
    slots()
    for i in (4, 8, 5):
        copies[i].wait()
    third = expand(wtb, z_third, 2, True)
    fourth = expand(wob, z_fourth, 2, True)
    layer(b_top, 384, 1, z_second, bs_ref, lambda a, v: put(b_mid, 0, a * 128, v), [(deeper, 3), (third, 3)])
    run(deeper)
    run(third)
    layer(b_mid, 0, 2, z_third, bt_ref, lambda a, v: put(b_top, 0, a * 128, v), [(fourth, 3)])
    run(fourth)
    copies[9].wait()
    copies[10].wait()

    z_head[...] = jnp.zeros((16, 128), f32)
    head = hw_ref[...].astype(f32)
    for z in range(4):
        z_head[z * 3:z * 3 + 3, z * 32:z * 32 + 28] = head
    hweight = z_head[...].astype(bf16)
    hrow = lax.broadcasted_iota(jnp.int32, (16, 128), 0)
    hlane = lax.broadcasted_iota(jnp.int32, (16, 128), 1)
    kind = lax.rem(hrow, 3)
    hbias = jnp.where(kind == 0, hb_ref[0], jnp.where(kind == 1, hb_ref[1], hb_ref[2]))
    depth = jnp.where((hrow < 3) | (hrow >= 9), bump(0, 4), bump(1, 4))
    wave = jnp.sin((hlane.astype(f32) + 0.5) * (math.pi / 128))
    window = depth * (wave * wave)

    def keep(a, v):
        b_feat[0:128, a * 128:(a + 1) * 128] = v.astype(bf16)

    layer(b_top, 0, 2, z_fourth, bo_ref, keep)
    logits = jnp.dot(hweight, b_feat[0:128, :], preferred_element_type=f32)
    for a in range(12):
        value = jax.nn.sigmoid(logits[:, a * 128:(a + 1) * 128] + hbias) * (window * bump(a, 12))
        planes[pl.ds(3 + a, 12, stride=ROWS), :] = value[:12]


def kernel(feat, deep, wf, ws, wt, wo, bf_, bs, bt, bo, hw, hb, first_hbm, offset_hbm, out_ref,
           fbuf, dbuf, wfb, wsb, wtb, wob, bfb, bsb, btb, bob, hwb, hb_ref, first_ref, offset_ref,
           planes, plane, b_feat, b_mid, b_top, z_first, z_second, z_third, z_fourth, z_head,
           hot_ref, send_a, recv_a, pieces, send_b, recv_b, in_sem, sa_sem, ra_sem, sb_sem, rb_sem):
    seg = lax.axis_index("segment")
    patch = lax.axis_index("patch")
    half = lax.div(patch, 16)
    line = lax.rem(lax.div(patch, 4), 4)
    turn = lax.rem(patch, 4)
    here = half * 16 + turn * 4 + seg

    buffers = (fbuf, dbuf, wfb, wsb, wtb, wob, bfb, bsb, btb, bob, hwb)
    copies = copies_in(seg, (feat, deep, wf, ws, wt, wo, bf_, bs, bt, bo, hw), buffers, in_sem)
    tables = [pltpu.make_async_copy(src, dst, in_sem.at[11 + i]) for i, (src, dst) in enumerate(
        ((hb, hb_ref), (first_hbm, first_ref), (offset_hbm, offset_ref)))]
    for table in tables:
        table.start()

    halves = [half, 1 - half]
    turns = [lax.rem(turn + d, 4) for d in range(4)]
    segs = [lax.rem(seg + d, 4) for d in range(4)]
    lines = [lax.rem(line + d, 4) for d in range(4)]

    def device(h, y, t, s):
        return s * 32 + h * 16 + y * 4 + t

    others = [(h, t, s) for h in (1, 0) for t in (2, 1, 3, 0) for s in (2, 1, 3, 0) if h or t or s]
    ids = [device(halves[h], line, turns[t], segs[s]) for h, t, s in others]
    spots = [halves[h] * 16 + turns[t] * 4 + segs[s] for h, t, s in others]
    barrier = pltpu.get_barrier_semaphore()
    for peer in ids + [device(half, y, turn, seg) for y in lines[1:]]:
        pl.semaphore_signal(barrier, inc=1, device_id=peer, device_id_type=LOGICAL)

    def slots():
        for table in tables:
            table.wait()
        spot = lax.broadcasted_iota(jnp.int32, (32, 32), 1)
        rank = lax.broadcasted_iota(jnp.int32, (32, 32), 0)
        slot = jnp.zeros((32, 32), jnp.int32)
        for j in range(32):
            begin = first_ref[(j // 16 * 4 + line) * 16 + j % 16]
            block = begin + lax.rem(turn - begin + 256, 4)
            slot = jnp.where(spot == j, lax.div(block, 4), slot)
        goal = (rank % 8) * 8 + half * 4 + (rank // 8 + line) % 4
        hot_ref[...] = (slot == goal).astype(f32)

    convolve(copies, slots, buffers, hb_ref, planes, plane, b_feat, b_mid, b_top,
             z_first, z_second, z_third, z_fourth, z_head)

    own = patch * 4 + seg
    first = first_ref[own]
    shift = 3 - offset_ref[own]
    starts = [shift + 4 * lax.rem(t - first + 256, 4) for t in turns]
    pl.semaphore_wait(barrier, 34)

    def stage_a(n):
        h, t, s = others[n]
        return pltpu.make_async_remote_copy(
            src_ref=send_a.at[t * 4 + s], dst_ref=recv_a.at[here],
            send_sem=sa_sem.at[n], recv_sem=ra_sem.at[here],
            device_id=ids[n], device_id_type=LOGICAL)

    for n, (h, t, s) in enumerate(others):
        if h:
            base = segs[s] * (3 * ROWS) + starts[t]
            value = jnp.concatenate(
                [planes[pl.ds(base + kind * ROWS, 4), :] for kind in range(3)], axis=0)
            send_a[t * 4 + s] = (value * value).astype(bf16)
        stage_a(n).start()
    recv_a[here] = send_a[0]
    for n, (h, t, s) in enumerate(others):
        source = spots[others.index((h, (4 - t) % 4, (4 - s) % 4))]
        pltpu.make_async_remote_copy(
            src_ref=send_a.at[t * 4 + s], dst_ref=recv_a.at[source],
            send_sem=sa_sem.at[n], recv_sem=ra_sem.at[source],
            device_id=ids[n], device_id_type=LOGICAL).wait_recv()

    for j in range(32):
        pieces[16 * j:16 * j + 12, :] = jnp.sqrt(recv_a[j].astype(f32))
    hot = hot_ref[...].astype(bf16)
    hot = jnp.concatenate([hot, hot], axis=1)
    for r in range(12):
        x = pieces[pl.ds(r, 32, stride=16), :]
        high = x.astype(bf16)
        low = (x - high.astype(f32)).astype(bf16)
        v = jnp.dot(hot, jnp.concatenate([high, low], axis=0), preferred_element_type=f32)
        v = v * v
        send_b[:, :, r * 128:(r + 1) * 128] = (v * v).reshape(4, 8, 128).astype(bf16)

    stage_b = []
    for d in (2, 1, 3):
        copy = pltpu.make_async_remote_copy(
            src_ref=send_b.at[d], dst_ref=recv_b.at[d],
            send_sem=sb_sem.at[d], recv_sem=rb_sem.at[d],
            device_id=device(half, lines[d], turn, seg), device_id_type=LOGICAL)
        copy.start()
        stage_b.append(copy)

    def decode(x):
        return jnp.sqrt(jnp.sqrt(x.astype(f32)))

    total = decode(send_b[0])
    for copy in stage_b:
        copy.wait_recv()
    for d in range(1, 4):
        total = total + decode(recv_b[d])
    for r in range(12):
        out_ref[pl.ds(r, 8, stride=12), :] = total[:, r * 128:(r + 1) * 128]
    for n in range(31):
        stage_a(n).wait_send()
    for copy in stage_b:
        copy.wait_send()


def conv_buffers():
    V = pltpu.VMEM
    return [
        V((1344, 128), bf16), V((1344, 128), bf16),
        V((9, 28, 28), bf16), V((27, 28, 28), bf16), V((27, 28, 56), bf16), V((27, 28, 56), bf16),
        V((1, 28), f32), V((1, 28), f32), V((1, 28), f32), V((1, 28), f32), V((3, 28), bf16),
    ]


def conv_scratch():
    V = pltpu.VMEM
    return [
        V((1536, 128), f32),
        V((384, 1536), bf16), V((768, 1536), bf16), V((768, 1536), bf16),
        V((384, 384), bf16), V((384, 384), bf16), V((384, 768), bf16), V((384, 768), bf16),
        V((16, 128), f32),
    ]


def per_device(features, deep_path, weight_first, bias_first, weight_second, bias_second,
               weight_third, bias_third, weight_fourth, bias_fourth, head_weight, head_bias,
               block_first, block_offset):
    def rows(x):
        return x.transpose(0, 1, 3, 2, 4).reshape(4, 1344, 128)

    hbm = pl.BlockSpec(memory_space=pltpu.HBM)
    vmem = pl.BlockSpec(memory_space=pltpu.VMEM)
    V = pltpu.VMEM
    dma = pltpu.SemaphoreType.DMA
    blended = pl.pallas_call(
        kernel,
        out_shape=V((96, 128), f32),
        in_specs=[hbm] * 14,
        out_specs=vmem,
        scratch_shapes=conv_buffers() + [
            pltpu.SMEM((3,), f32), pltpu.SMEM((128,), jnp.int32), pltpu.SMEM((128,), jnp.int32),
            V((12 * ROWS, 128), f32)] + conv_scratch() + [
            V((32, 32), f32), V((16, 12, 128), bf16), V((32, 12, 128), bf16), V((512, 128), f32),
            V((4, 8, 1536), bf16), V((4, 8, 1536), bf16),
            dma((14,)), dma((31,)), dma((32,)), dma((4,)), dma((4,)),
        ],
        compiler_params=pltpu.CompilerParams(
            collective_id=0, has_side_effects=True, vmem_limit_bytes=60 << 20),
    )(rows(features), rows(deep_path), weight_first, weight_second, weight_third, weight_fourth,
      bias_first.reshape(1, 28), bias_second.reshape(1, 28), bias_third.reshape(1, 28),
      bias_fourth.reshape(1, 28), head_weight, head_bias, block_first, block_offset)
    return blended.reshape(8, 1, 3, 1, 4, 128)


def solution(mesh):
    placed = (P("patch"), P("patch")) + (P(),) * 12
    return jax.shard_map(
        per_device,
        mesh=mesh,
        in_specs=placed,
        out_specs=P(None, "patch", None, "segment", None, None),
        check_vma=False,
    )
```

```python
import math

import jax
import jax.numpy as jnp
from jax import lax
from jax.experimental import pallas as pl
from jax.experimental.pallas import tpu as pltpu
from jax.sharding import PartitionSpec as P

bf16 = jnp.bfloat16
f32 = jnp.float32
LOGICAL = pl.DeviceIdType.LOGICAL
ROWS = 24


def bump(n, length):
    return math.sin(math.pi * (n + 0.5) / length) ** 2


def copies_in(s, hbm, buffers, sems):
    sources = [ref.at[s] if i < 2 else ref for i, ref in enumerate(hbm)]
    copies = [pltpu.make_async_copy(src, dst, sems.at[i])
              for i, (src, dst) in enumerate(zip(sources, buffers))]
    for i in (2, 0, 6, 3, 7, 1, 4, 8, 5, 9, 10):
        copies[i].start()
    return copies


def convolve(copies, slots, buffers, hb_ref, planes, plane, b_feat, b_mid, b_top,
             z_first, z_second, z_third, z_fourth, z_head):
    fbuf, dbuf, wfb, wsb, wtb, wob, bf_ref, bs_ref, bt_ref, bo_ref, hw_ref = buffers

    plane[1344:1536, :] = jnp.zeros((192, 128), f32)
    planes[...] = jnp.zeros(planes.shape, f32)
    for dst in (z_first, z_second, z_third, z_fourth):
        dst[...] = jnp.zeros(dst.shape, bf16)
    lane = lax.broadcasted_iota(jnp.int32, (128, 128), 1)

    def put(buf, row0, col0, v):
        v = v.astype(bf16)
        zero = jnp.zeros((128, 128), bf16)
        buf[row0:row0 + 128, col0:col0 + 128] = jnp.where(lane > 0, pltpu.roll(v, 1, 1), zero)
        buf[row0 + 128:row0 + 256, col0:col0 + 128] = v
        buf[row0 + 256:row0 + 384, col0:col0 + 128] = jnp.where(lane < 127, pltpu.roll(v, 127, 1), zero)

    def relayout(src, buf, row0):
        for c in range(0, 1344, 336):
            plane[c:c + 336, :] = src[c:c + 336, :].astype(f32)
            yield
        for a in range(12):
            cell = [plane[pl.ds(4 * a + z, 32, stride=48), :] for z in range(4)]
            put(buf, row0, a * 128, jnp.concatenate(cell, axis=0))
            yield

    def expand(w, dst, parts, full):
        for t in range(9):
            da, dy = t // 3, t % 3
            for part in range(parts):
                base = (part * 3 + dy) * 128
                for zo in range(4):
                    for zi in range(4):
                        if abs(zi - zo) > (1 if full else 0):
                            continue
                        tap = 9 * (zi - zo + 1) + t if full else t
                        dst[da * 128 + zo * 32:da * 128 + zo * 32 + 28, base + zi * 32:base + zi * 32 + 28] = (
                            w[tap, :, part * 28:part * 28 + 28])
                yield

    def column(ref):
        lanes = lax.broadcasted_iota(jnp.int32, (128, 28), 1)
        rows = lax.rem(lax.broadcasted_iota(jnp.int32, (128, 28), 0), 32)
        return jnp.sum(jnp.where(lanes == rows, ref[...], 0.0), axis=1, keepdims=True)

    def layer(src, row0, parts, weights, bias_ref, emit, beside=()):
        k = parts * 384
        bias = column(bias_ref)
        sums = {}
        for n in range(6):
            p = jnp.dot(weights[...], src[row0:row0 + k, n * 256:(n + 1) * 256],
                        preferred_element_type=f32)
            for task, count in beside:
                for _ in range(count):
                    next(task, None)
            settle()
            for b in (2 * n, 2 * n + 1):
                for da in (2, 1, 0):
                    a = b + 1 - da
                    if 0 <= a < 12:
                        term = p[da * 128:(da + 1) * 128, (b - 2 * n) * 128:(b - 2 * n + 1) * 128]
                        sums[a] = sums[a] + term if a in sums else term
            for a in (2 * n - 1, 2 * n) + ((11,) if n == 5 else ()):
                if a >= 0:
                    pending.append((emit, a, sums.pop(a), bias))

    pending = []

    def settle():
        while pending:
            emit, a, total, bias = pending.pop(0)
            emit(a, jnp.maximum(total + bias, 0.0))

    def run(task):
        for _ in task:
            pass

    copies[2].wait()
    run(expand(wfb, z_first, 1, False))
    copies[0].wait()
    run(relayout(fbuf, b_feat, 0))
    slots()
    for i in (6, 3, 7, 1, 4, 8, 5, 9, 10):
        copies[i].wait()
    second = expand(wsb, z_second, 1, True)
    deeper = relayout(dbuf, b_mid, 384)
    layer(b_feat, 0, 1, z_first, bf_ref, lambda a, v: put(b_top, 384, a * 128, v), [(second, 2), (deeper, 2)])
    run(second)
    third = expand(wtb, z_third, 2, True)
    fourth = expand(wob, z_fourth, 2, True)
    layer(b_top, 384, 1, z_second, bs_ref, lambda a, v: put(b_mid, 0, a * 128, v), [(deeper, 3), (third, 3)])
    run(deeper)
    run(third)
    layer(b_mid, 0, 2, z_third, bt_ref, lambda a, v: put(b_top, 0, a * 128, v), [(fourth, 3)])
    run(fourth)

    z_head[...] = jnp.zeros((16, 128), f32)
    head = hw_ref[...].astype(f32)
    for z in range(4):
        z_head[z * 3:z * 3 + 3, z * 32:z * 32 + 28] = head
    hweight = z_head[...].astype(bf16)
    hrow = lax.broadcasted_iota(jnp.int32, (16, 128), 0)
    hlane = lax.broadcasted_iota(jnp.int32, (16, 128), 1)
    kind = lax.rem(hrow, 3)
    hbias = jnp.where(kind == 0, hb_ref[0], jnp.where(kind == 1, hb_ref[1], hb_ref[2]))
    depth = jnp.where((hrow < 3) | (hrow >= 9), bump(0, 4), bump(1, 4))
    wave = jnp.sin((hlane.astype(f32) + 0.5) * (math.pi / 128))
    window = depth * (wave * wave)

    def keep(a, v):
        b_feat[0:128, a * 128:(a + 1) * 128] = v.astype(bf16)

    layer(b_top, 0, 2, z_fourth, bo_ref, keep)
    settle()
    logits = jnp.dot(hweight, b_feat[0:128, :], preferred_element_type=f32)
    for a in range(12):
        value = jax.nn.sigmoid(logits[:, a * 128:(a + 1) * 128] + hbias) * (window * bump(a, 12))
        planes[pl.ds(3 + a, 12, stride=ROWS), :] = value[:12]


def kernel(feat, deep, wf, ws, wt, wo, bf_, bs, bt, bo, hw, hb, first_hbm, offset_hbm, out_ref,
           fbuf, dbuf, wfb, wsb, wtb, wob, bfb, bsb, btb, bob, hwb, hb_ref, first_ref, offset_ref,
           planes, plane, b_feat, b_mid, b_top, z_first, z_second, z_third, z_fourth, z_head,
           hot_ref, send_a, recv_a, pieces, send_b, recv_b, in_sem, sa_sem, ra_sem, sb_sem, rb_sem):
    seg = lax.axis_index("segment")
    patch = lax.axis_index("patch")
    half = lax.div(patch, 16)
    line = lax.rem(lax.div(patch, 4), 4)
    turn = lax.rem(patch, 4)
    here = half * 16 + turn * 4 + seg

    buffers = (fbuf, dbuf, wfb, wsb, wtb, wob, bfb, bsb, btb, bob, hwb)
    copies = copies_in(seg, (feat, deep, wf, ws, wt, wo, bf_, bs, bt, bo, hw), buffers, in_sem)
    tables = [pltpu.make_async_copy(src, dst, in_sem.at[11 + i]) for i, (src, dst) in enumerate(
        ((hb, hb_ref), (first_hbm, first_ref), (offset_hbm, offset_ref)))]
    for table in tables:
        table.start()

    halves = [half, 1 - half]
    turns = [lax.rem(turn + d, 4) for d in range(4)]
    segs = [lax.rem(seg + d, 4) for d in range(4)]
    lines = [lax.rem(line + d, 4) for d in range(4)]

    def device(h, y, t, s):
        return s * 32 + h * 16 + y * 4 + t

    others = [(h, t, s) for h in (1, 0) for t in (2, 1, 3, 0) for s in (2, 1, 3, 0) if h or t or s]
    ids = [device(halves[h], line, turns[t], segs[s]) for h, t, s in others]
    spots = [halves[h] * 16 + turns[t] * 4 + segs[s] for h, t, s in others]
    barrier = pltpu.get_barrier_semaphore()
    for peer in ids + [device(half, y, turn, seg) for y in lines[1:]]:
        pl.semaphore_signal(barrier, inc=1, device_id=peer, device_id_type=LOGICAL)

    def slots():
        for table in tables:
            table.wait()
        spot = lax.broadcasted_iota(jnp.int32, (32, 32), 1)
        rank = lax.broadcasted_iota(jnp.int32, (32, 32), 0)
        slot = jnp.zeros((32, 32), jnp.int32)
        for j in range(32):
            begin = first_ref[(j // 16 * 4 + line) * 16 + j % 16]
            block = begin + lax.rem(turn - begin + 256, 4)
            slot = jnp.where(spot == j, lax.div(block, 4), slot)
        goal = (rank % 8) * 8 + half * 4 + (rank // 8 + line) % 4
        hot_ref[...] = (slot == goal).astype(f32)

    convolve(copies, slots, buffers, hb_ref, planes, plane, b_feat, b_mid, b_top,
             z_first, z_second, z_third, z_fourth, z_head)

    own = patch * 4 + seg
    first = first_ref[own]
    shift = 3 - offset_ref[own]
    starts = [shift + 4 * lax.rem(t - first + 256, 4) for t in turns]
    pl.semaphore_wait(barrier, 34)

    def stage_a(n):
        h, t, s = others[n]
        return pltpu.make_async_remote_copy(
            src_ref=send_a.at[t * 4 + s], dst_ref=recv_a.at[here],
            send_sem=sa_sem.at[n], recv_sem=ra_sem.at[here],
            device_id=ids[n], device_id_type=LOGICAL)

    for n, (h, t, s) in enumerate(others):
        if h:
            base = segs[s] * (3 * ROWS) + starts[t]
            value = jnp.concatenate(
                [planes[pl.ds(base + kind * ROWS, 4), :] for kind in range(3)], axis=0)
            send_a[t * 4 + s] = (value * value).astype(bf16)
        stage_a(n).start()
    recv_a[here] = send_a[0]
    for n, (h, t, s) in enumerate(others):
        source = spots[others.index((h, (4 - t) % 4, (4 - s) % 4))]
        pltpu.make_async_remote_copy(
            src_ref=send_a.at[t * 4 + s], dst_ref=recv_a.at[source],
            send_sem=sa_sem.at[n], recv_sem=ra_sem.at[source],
            device_id=ids[n], device_id_type=LOGICAL).wait_recv()

    for j in range(32):
        pieces[16 * j:16 * j + 12, :] = jnp.sqrt(recv_a[j].astype(f32))
    hot = hot_ref[...].astype(bf16)
    hot = jnp.concatenate([hot, hot], axis=1)
    for r in range(12):
        x = pieces[pl.ds(r, 32, stride=16), :]
        high = x.astype(bf16)
        low = (x - high.astype(f32)).astype(bf16)
        v = jnp.dot(hot, jnp.concatenate([high, low], axis=0), preferred_element_type=f32)
        v = v * v
        send_b[:, :, r * 128:(r + 1) * 128] = (v * v).reshape(4, 8, 128).astype(bf16)

    stage_b = []
    for d in (2, 1, 3):
        copy = pltpu.make_async_remote_copy(
            src_ref=send_b.at[d], dst_ref=recv_b.at[d],
            send_sem=sb_sem.at[d], recv_sem=rb_sem.at[d],
            device_id=device(half, lines[d], turn, seg), device_id_type=LOGICAL)
        copy.start()
        stage_b.append(copy)

    def decode(x):
        return jnp.sqrt(jnp.sqrt(x.astype(f32)))

    for n in range(31):
        stage_a(n).wait_send()
    total = decode(send_b[0])
    for copy in stage_b:
        copy.wait_recv()
    for d in range(1, 4):
        total = total + decode(recv_b[d])
    for r in range(12):
        out_ref[pl.ds(r, 8, stride=12), :] = total[:, r * 128:(r + 1) * 128]
    for copy in stage_b:
        copy.wait_send()


def conv_buffers():
    V = pltpu.VMEM
    return [
        V((1344, 128), bf16), V((1344, 128), bf16),
        V((9, 28, 28), bf16), V((27, 28, 28), bf16), V((27, 28, 56), bf16), V((27, 28, 56), bf16),
        V((1, 28), f32), V((1, 28), f32), V((1, 28), f32), V((1, 28), f32), V((3, 28), bf16),
    ]


def conv_scratch():
    V = pltpu.VMEM
    return [
        V((1536, 128), f32),
        V((384, 1536), bf16), V((768, 1536), bf16), V((768, 1536), bf16),
        V((384, 384), bf16), V((384, 384), bf16), V((384, 768), bf16), V((384, 768), bf16),
        V((16, 128), f32),
    ]


def per_device(features, deep_path, weight_first, bias_first, weight_second, bias_second,
               weight_third, bias_third, weight_fourth, bias_fourth, head_weight, head_bias,
               block_first, block_offset):
    def rows(x):
        return x.transpose(0, 1, 3, 2, 4).reshape(4, 1344, 128)

    hbm = pl.BlockSpec(memory_space=pltpu.HBM)
    vmem = pl.BlockSpec(memory_space=pltpu.VMEM)
    V = pltpu.VMEM
    dma = pltpu.SemaphoreType.DMA
    blended = pl.pallas_call(
        kernel,
        out_shape=V((96, 128), f32),
        in_specs=[hbm] * 14,
        out_specs=vmem,
        scratch_shapes=conv_buffers() + [
            pltpu.SMEM((3,), f32), pltpu.SMEM((128,), jnp.int32), pltpu.SMEM((128,), jnp.int32),
            V((12 * ROWS, 128), f32)] + conv_scratch() + [
            V((32, 32), f32), V((16, 12, 128), bf16), V((32, 12, 128), bf16), V((512, 128), f32),
            V((4, 8, 1536), bf16), V((4, 8, 1536), bf16),
            dma((14,)), dma((31,)), dma((32,)), dma((4,)), dma((4,)),
        ],
        compiler_params=pltpu.CompilerParams(
            collective_id=0, has_side_effects=True, vmem_limit_bytes=60 << 20),
    )(rows(features), rows(deep_path), weight_first, weight_second, weight_third, weight_fourth,
      bias_first.reshape(1, 28), bias_second.reshape(1, 28), bias_third.reshape(1, 28),
      bias_fourth.reshape(1, 28), head_weight, head_bias, block_first, block_offset)
    return blended.reshape(8, 1, 3, 1, 4, 128)


def solution(mesh):
    placed = (P("patch"), P("patch")) + (P(),) * 12
    return jax.shard_map(
        per_device,
        mesh=mesh,
        in_specs=placed,
        out_specs=P(None, "patch", None, "segment", None, None),
        check_vma=False,
    )
```

```python
import math

import jax
import jax.numpy as jnp
from jax import lax
from jax.experimental import pallas as pl
from jax.experimental.pallas import tpu as pltpu
from jax.sharding import PartitionSpec as P

bf16 = jnp.bfloat16
f32 = jnp.float32
LOGICAL = pl.DeviceIdType.LOGICAL
ROWS = 24


def bump(n, length):
    return math.sin(math.pi * (n + 0.5) / length) ** 2


def copies_in(s, hbm, buffers, sems):
    sources = [ref.at[s] if i < 2 else ref for i, ref in enumerate(hbm)]
    for w in buffers[2:6]:
        w[:, 16:32, :] = jnp.zeros((w.shape[0], 16, w.shape[2]), bf16)
    buffers = [w.at[:, 0:28, :] if 1 < i < 6 else w for i, w in enumerate(buffers)]
    copies = [pltpu.make_async_copy(src, dst, sems.at[i])
              for i, (src, dst) in enumerate(zip(sources, buffers))]
    for i in (2, 0, 6, 3, 7, 1, 4, 8, 5, 9, 10):
        copies[i].start()
    return copies


def convolve(copies, slots, buffers, hb_ref, planes, plane, b_feat, b_mid, b_top,
             z_first, z_second, z_third, z_fourth, z_head):
    fbuf, dbuf, wfb, wsb, wtb, wob, bf_ref, bs_ref, bt_ref, bo_ref, hw_ref = buffers

    plane[1344:1536, :] = jnp.zeros((192, 128), f32)
    planes[...] = jnp.zeros(planes.shape, f32)
    for dst in (z_first, z_second, z_third, z_fourth):
        dst[...] = jnp.zeros(dst.shape, bf16)
    lane = lax.broadcasted_iota(jnp.int32, (128, 128), 1)

    def put(buf, row0, col0, v):
        v = v.astype(bf16)
        zero = jnp.zeros((128, 128), bf16)
        buf[row0:row0 + 128, col0:col0 + 128] = jnp.where(lane > 0, pltpu.roll(v, 1, 1), zero)
        buf[row0 + 128:row0 + 256, col0:col0 + 128] = v
        buf[row0 + 256:row0 + 384, col0:col0 + 128] = jnp.where(lane < 127, pltpu.roll(v, 127, 1), zero)

    def relayout(src, buf, row0):
        for c in range(0, 1344, 336):
            plane[c:c + 336, :] = src[c:c + 336, :].astype(f32)
            yield
        for a in range(12):
            cell = [plane[pl.ds(4 * a + z, 32, stride=48), :] for z in range(4)]
            put(buf, row0, a * 128, jnp.concatenate(cell, axis=0))
            yield

    def expand(w, dst, parts, full):
        for t in range(9):
            da, dy = t // 3, t % 3
            for part in range(parts):
                base = (part * 3 + dy) * 128
                for zo in range(4):
                    for zi in range(4):
                        if abs(zi - zo) > (1 if full else 0):
                            continue
                        tap = 9 * (zi - zo + 1) + t if full else t
                        dst[da * 128 + zo * 32:da * 128 + zo * 32 + 32, base + zi * 32:base + zi * 32 + 28] = (
                            w[tap, :, part * 28:part * 28 + 28])
                yield

    def column(ref):
        lanes = lax.broadcasted_iota(jnp.int32, (128, 28), 1)
        rows = lax.rem(lax.broadcasted_iota(jnp.int32, (128, 28), 0), 32)
        return jnp.sum(jnp.where(lanes == rows, ref[...], 0.0), axis=1, keepdims=True)

    def layer(src, row0, parts, weights, bias_ref, emit, beside=()):
        k = parts * 384
        bias = column(bias_ref)
        sums = {}
        for n in range(6):
            p = jnp.dot(weights[...], src[row0:row0 + k, n * 256:(n + 1) * 256],
                        preferred_element_type=f32)
            for task, count in beside:
                for _ in range(count):
                    next(task, None)
            settle()
            for b in (2 * n, 2 * n + 1):
                for da in (2, 1, 0):
                    a = b + 1 - da
                    if 0 <= a < 12:
                        term = p[da * 128:(da + 1) * 128, (b - 2 * n) * 128:(b - 2 * n + 1) * 128]
                        sums[a] = sums[a] + term if a in sums else term
            for a in (2 * n - 1, 2 * n) + ((11,) if n == 5 else ()):
                if a >= 0:
                    pending.append((emit, a, sums.pop(a), bias))

    pending = []

    def settle():
        while pending:
            emit, a, total, bias = pending.pop(0)
            emit(a, jnp.maximum(total + bias, 0.0))

    def run(task):
        for _ in task:
            pass

    copies[2].wait()
    run(expand(wfb, z_first, 1, False))
    copies[0].wait()
    run(relayout(fbuf, b_feat, 0))
    slots()
    for i in (6, 3, 7, 1, 4, 8, 5, 9, 10):
        copies[i].wait()
    second = expand(wsb, z_second, 1, True)
    deeper = relayout(dbuf, b_mid, 384)
    layer(b_feat, 0, 1, z_first, bf_ref, lambda a, v: put(b_top, 384, a * 128, v), [(second, 2), (deeper, 2)])
    run(second)
    third = expand(wtb, z_third, 2, True)
    fourth = expand(wob, z_fourth, 2, True)
    layer(b_top, 384, 1, z_second, bs_ref, lambda a, v: put(b_mid, 0, a * 128, v), [(deeper, 3), (third, 3)])
    run(deeper)
    run(third)
    layer(b_mid, 0, 2, z_third, bt_ref, lambda a, v: put(b_top, 0, a * 128, v), [(fourth, 3)])
    run(fourth)

    z_head[...] = jnp.zeros((16, 128), f32)
    head = hw_ref[...].astype(f32)
    for z in range(4):
        z_head[z * 3:z * 3 + 3, z * 32:z * 32 + 28] = head
    hweight = z_head[...].astype(bf16)
    hrow = lax.broadcasted_iota(jnp.int32, (16, 128), 0)
    hlane = lax.broadcasted_iota(jnp.int32, (16, 128), 1)
    kind = lax.rem(hrow, 3)
    hbias = jnp.where(kind == 0, hb_ref[0], jnp.where(kind == 1, hb_ref[1], hb_ref[2]))
    depth = jnp.where((hrow < 3) | (hrow >= 9), bump(0, 4), bump(1, 4))
    wave = jnp.sin((hlane.astype(f32) + 0.5) * (math.pi / 128))
    window = depth * (wave * wave)

    def keep(a, v):
        b_feat[0:128, a * 128:(a + 1) * 128] = v.astype(bf16)

    layer(b_top, 0, 2, z_fourth, bo_ref, keep)
    settle()
    logits = jnp.dot(hweight, b_feat[0:128, :], preferred_element_type=f32)
    for a in range(12):
        value = jax.nn.sigmoid(logits[:, a * 128:(a + 1) * 128] + hbias) * (window * bump(a, 12))
        planes[pl.ds(3 + a, 12, stride=ROWS), :] = value[:12]


def kernel(feat, deep, wf, ws, wt, wo, bf_, bs, bt, bo, hw, hb, first_hbm, offset_hbm, out_ref,
           fbuf, dbuf, wfb, wsb, wtb, wob, bfb, bsb, btb, bob, hwb, hb_ref, first_ref, offset_ref,
           planes, plane, b_feat, b_mid, b_top, z_first, z_second, z_third, z_fourth, z_head,
           hot_ref, send_a, recv_a, pieces, send_b, recv_b, in_sem, sa_sem, ra_sem, sb_sem, rb_sem):
    seg = lax.axis_index("segment")
    patch = lax.axis_index("patch")
    half = lax.div(patch, 16)
    line = lax.rem(lax.div(patch, 4), 4)
    turn = lax.rem(patch, 4)
    here = half * 16 + turn * 4 + seg

    buffers = (fbuf, dbuf, wfb, wsb, wtb, wob, bfb, bsb, btb, bob, hwb)
    copies = copies_in(seg, (feat, deep, wf, ws, wt, wo, bf_, bs, bt, bo, hw), buffers, in_sem)
    tables = [pltpu.make_async_copy(src, dst, in_sem.at[11 + i]) for i, (src, dst) in enumerate(
        ((hb, hb_ref), (first_hbm, first_ref), (offset_hbm, offset_ref)))]
    for table in tables:
        table.start()

    halves = [half, 1 - half]
    turns = [lax.rem(turn + d, 4) for d in range(4)]
    segs = [lax.rem(seg + d, 4) for d in range(4)]
    lines = [lax.rem(line + d, 4) for d in range(4)]

    def device(h, y, t, s):
        return s * 32 + h * 16 + y * 4 + t

    others = [(h, t, s) for h in (1, 0) for t in (2, 1, 3, 0) for s in (2, 1, 3, 0) if h or t or s]
    ids = [device(halves[h], line, turns[t], segs[s]) for h, t, s in others]
    barrier = pltpu.get_barrier_semaphore()
    for peer in ids + [device(half, y, turn, seg) for y in lines[1:]]:
        pl.semaphore_signal(barrier, inc=1, device_id=peer, device_id_type=LOGICAL)

    def slots():
        for table in tables:
            table.wait()
        spot = lax.broadcasted_iota(jnp.int32, (32, 32), 1)
        rank = lax.broadcasted_iota(jnp.int32, (32, 32), 0)
        slot = jnp.zeros((32, 32), jnp.int32)
        for j in range(32):
            begin = first_ref[(j // 16 * 4 + line) * 16 + j % 16]
            block = begin + lax.rem(turn - begin + 256, 4)
            slot = jnp.where(spot == j, lax.div(block, 4), slot)
        goal = (rank % 8) * 8 + half * 4 + (rank // 8 + line) % 4
        hot_ref[...] = (slot == goal).astype(f32)

    convolve(copies, slots, buffers, hb_ref, planes, plane, b_feat, b_mid, b_top,
             z_first, z_second, z_third, z_fourth, z_head)

    own = patch * 4 + seg
    first = first_ref[own]
    shift = 3 - offset_ref[own]
    starts = [shift + 4 * lax.rem(t - first + 256, 4) for t in turns]
    pl.semaphore_wait(barrier, 34)

    def stage_a(n):
        h, t, s = others[n]
        return pltpu.make_async_remote_copy(
            src_ref=send_a.at[t * 4 + s], dst_ref=recv_a.at[here],
            send_sem=sa_sem, recv_sem=ra_sem,
            device_id=ids[n], device_id_type=LOGICAL)

    for n, (h, t, s) in enumerate(others):
        if h:
            base = segs[s] * (3 * ROWS) + starts[t]
            value = jnp.concatenate(
                [planes[pl.ds(base + kind * ROWS, 4), :] for kind in range(3)], axis=0)
            send_a[t * 4 + s] = (value * value).astype(bf16)
        stage_a(n).start()
    recv_a[here] = send_a[0]
    def all_pieces(ref, sem):
        return pltpu.make_async_copy(ref.at[pl.ds(0, 31)], ref.at[pl.ds(0, 31)], sem)

    all_pieces(recv_a, ra_sem).wait()

    for j in range(32):
        pieces[16 * j:16 * j + 12, :] = jnp.sqrt(recv_a[j].astype(f32))
    hot = hot_ref[...].astype(bf16)
    hot = jnp.concatenate([hot, hot], axis=1)
    for r in range(12):
        x = pieces[pl.ds(r, 32, stride=16), :]
        high = x.astype(bf16)
        low = (x - high.astype(f32)).astype(bf16)
        v = jnp.dot(hot, jnp.concatenate([high, low], axis=0), preferred_element_type=f32)
        v = v * v
        send_b[:, :, r * 128:(r + 1) * 128] = (v * v).reshape(4, 8, 128).astype(bf16)

    stage_b = []
    for d in (2, 1, 3):
        copy = pltpu.make_async_remote_copy(
            src_ref=send_b.at[d], dst_ref=recv_b.at[d],
            send_sem=sb_sem.at[d], recv_sem=rb_sem.at[d],
            device_id=device(half, lines[d], turn, seg), device_id_type=LOGICAL)
        copy.start()
        stage_b.append(copy)

    def decode(x):
        return jnp.sqrt(jnp.sqrt(x.astype(f32)))

    all_pieces(recv_a, sa_sem).wait()
    total = decode(send_b[0])
    for copy in stage_b:
        copy.wait_recv()
    for d in range(1, 4):
        total = total + decode(recv_b[d])
    for r in range(12):
        out_ref[pl.ds(r, 8, stride=12), :] = total[:, r * 128:(r + 1) * 128]
    for copy in stage_b:
        copy.wait_send()


def conv_buffers():
    V = pltpu.VMEM
    return [
        V((1344, 128), bf16), V((1344, 128), bf16),
        V((9, 32, 28), bf16), V((27, 32, 28), bf16), V((27, 32, 56), bf16), V((27, 32, 56), bf16),
        V((1, 28), f32), V((1, 28), f32), V((1, 28), f32), V((1, 28), f32), V((3, 28), bf16),
    ]


def conv_scratch():
    V = pltpu.VMEM
    return [
        V((1536, 128), f32),
        V((384, 1536), bf16), V((768, 1536), bf16), V((768, 1536), bf16),
        V((384, 384), bf16), V((384, 384), bf16), V((384, 768), bf16), V((384, 768), bf16),
        V((16, 128), f32),
    ]


def per_device(features, deep_path, weight_first, bias_first, weight_second, bias_second,
               weight_third, bias_third, weight_fourth, bias_fourth, head_weight, head_bias,
               block_first, block_offset):
    def rows(x):
        return x.transpose(0, 1, 3, 2, 4).reshape(4, 1344, 128)

    hbm = pl.BlockSpec(memory_space=pltpu.HBM)
    vmem = pl.BlockSpec(memory_space=pltpu.VMEM)
    V = pltpu.VMEM
    dma = pltpu.SemaphoreType.DMA
    blended = pl.pallas_call(
        kernel,
        out_shape=V((96, 128), f32),
        in_specs=[hbm] * 14,
        out_specs=vmem,
        scratch_shapes=conv_buffers() + [
            pltpu.SMEM((3,), f32), pltpu.SMEM((128,), jnp.int32), pltpu.SMEM((128,), jnp.int32),
            V((12 * ROWS, 128), f32)] + conv_scratch() + [
            V((32, 32), f32), V((16, 12, 128), bf16), V((32, 12, 128), bf16), V((512, 128), f32),
            V((4, 8, 1536), bf16), V((4, 8, 1536), bf16),
            dma((14,)), dma(()), dma(()), dma((4,)), dma((4,)),
        ],
        compiler_params=pltpu.CompilerParams(
            collective_id=0, has_side_effects=True, vmem_limit_bytes=60 << 20),
    )(rows(features), rows(deep_path), weight_first, weight_second, weight_third, weight_fourth,
      bias_first.reshape(1, 28), bias_second.reshape(1, 28), bias_third.reshape(1, 28),
      bias_fourth.reshape(1, 28), head_weight, head_bias, block_first, block_offset)
    return blended.reshape(8, 1, 3, 1, 4, 128)


def solution(mesh):
    placed = (P("patch"), P("patch")) + (P(),) * 12
    return jax.shard_map(
        per_device,
        mesh=mesh,
        in_specs=placed,
        out_specs=P(None, "patch", None, "segment", None, None),
        check_vma=False,
    )
```

```python
import math

import jax
import jax.numpy as jnp
from jax import lax
from jax.experimental import pallas as pl
from jax.experimental.pallas import tpu as pltpu
from jax.sharding import PartitionSpec as P

bf16 = jnp.bfloat16
f32 = jnp.float32
LOGICAL = pl.DeviceIdType.LOGICAL
ROWS = 24


def bump(n, length):
    return math.sin(math.pi * (n + 0.5) / length) ** 2


def copies_in(s, hbm, buffers, sems):
    sources = [ref.at[s] if i < 2 else ref for i, ref in enumerate(hbm)]
    for w in buffers[2:6]:
        w[:, 16:32, :] = jnp.zeros((w.shape[0], 16, w.shape[2]), bf16)
    buffers = [w.at[:, 0:28, :] if 1 < i < 6 else w for i, w in enumerate(buffers)]
    copies = [pltpu.make_async_copy(src, dst, sems.at[i])
              for i, (src, dst) in enumerate(zip(sources, buffers))]
    for i in (2, 0, 6, 3, 7, 1, 4, 8, 5, 9, 10):
        copies[i].start()
    return copies


def convolve(copies, slots, buffers, hb_ref, planes, plane, b_feat, b_mid, b_top,
             z_first, z_second, z_third, z_fourth, z_head):
    fbuf, dbuf, wfb, wsb, wtb, wob, bf_ref, bs_ref, bt_ref, bo_ref, hw_ref = buffers

    plane[1344:1536, :] = jnp.zeros((192, 128), f32)
    planes[...] = jnp.zeros(planes.shape, f32)
    for dst in (z_first, z_second, z_third, z_fourth):
        dst[...] = jnp.zeros(dst.shape, bf16)
    lane = lax.broadcasted_iota(jnp.int32, (128, 128), 1)

    def put(buf, row0, col0, v):
        v = v.astype(bf16)
        zero = jnp.zeros((128, 128), bf16)
        buf[row0:row0 + 128, col0:col0 + 128] = jnp.where(lane > 0, pltpu.roll(v, 1, 1), zero)
        buf[row0 + 128:row0 + 256, col0:col0 + 128] = v
        buf[row0 + 256:row0 + 384, col0:col0 + 128] = jnp.where(lane < 127, pltpu.roll(v, 127, 1), zero)

    def relayout(src, buf, row0):
        for c in range(0, 1344, 336):
            plane[c:c + 336, :] = src[c:c + 336, :].astype(f32)
            yield
        for a in range(12):
            cell = [plane[pl.ds(4 * a + z, 32, stride=48), :] for z in range(4)]
            put(buf, row0, a * 128, jnp.concatenate(cell, axis=0))
            yield

    def expand(w, dst, parts, full):
        for t in range(9):
            da, dy = t // 3, t % 3
            for part in range(parts):
                base = (part * 3 + dy) * 128
                for zo in range(4):
                    for zi in range(4):
                        if abs(zi - zo) > (1 if full else 0):
                            continue
                        tap = 9 * (zi - zo + 1) + t if full else t
                        dst[da * 128 + zo * 32:da * 128 + zo * 32 + 32, base + zi * 32:base + zi * 32 + 28] = (
                            w[tap, :, part * 28:part * 28 + 28])
                yield

    def column(ref):
        lanes = lax.broadcasted_iota(jnp.int32, (128, 28), 1)
        rows = lax.rem(lax.broadcasted_iota(jnp.int32, (128, 28), 0), 32)
        return jnp.sum(jnp.where(lanes == rows, ref[...], 0.0), axis=1, keepdims=True)

    def layer(src, row0, parts, weights, bias_ref, emit, beside=()):
        k = parts * 384
        bias = column(bias_ref)
        sums = {}
        for n in range(6):
            p = jnp.dot(weights[...], src[row0:row0 + k, n * 256:(n + 1) * 256],
                        preferred_element_type=f32)
            for task, count in beside:
                for _ in range(count):
                    next(task, None)
            settle()
            for b in (2 * n, 2 * n + 1):
                for da in (2, 1, 0):
                    a = b + 1 - da
                    if 0 <= a < 12:
                        term = p[da * 128:(da + 1) * 128, (b - 2 * n) * 128:(b - 2 * n + 1) * 128]
                        sums[a] = sums[a] + term if a in sums else term
            for a in (2 * n - 1, 2 * n) + ((11,) if n == 5 else ()):
                if a >= 0:
                    pending.append((emit, a, sums.pop(a), bias))

    pending = []

    def settle():
        while pending:
            emit, a, total, bias = pending.pop(0)
            emit(a, jnp.maximum(total + bias, 0.0))

    def run(task):
        for _ in task:
            pass

    copies[2].wait()
    run(expand(wfb, z_first, 1, False))
    copies[0].wait()
    run(relayout(fbuf, b_feat, 0))
    slots()
    for i in (6, 3, 7, 1, 4, 8, 5, 9, 10):
        copies[i].wait()
    second = expand(wsb, z_second, 1, True)
    deeper = relayout(dbuf, b_mid, 384)
    layer(b_feat, 0, 1, z_first, bf_ref, lambda a, v: put(b_top, 384, a * 128, v), [(second, 2), (deeper, 2)])
    run(second)
    third = expand(wtb, z_third, 2, True)
    fourth = expand(wob, z_fourth, 2, True)
    layer(b_top, 384, 1, z_second, bs_ref, lambda a, v: put(b_mid, 0, a * 128, v), [(deeper, 3), (third, 3)])
    run(deeper)
    run(third)
    layer(b_mid, 0, 2, z_third, bt_ref, lambda a, v: put(b_top, 0, a * 128, v), [(fourth, 3)])
    run(fourth)

    z_head[...] = jnp.zeros((16, 128), f32)
    head = hw_ref[...].astype(f32)
    for z in range(4):
        z_head[z * 3:z * 3 + 3, z * 32:z * 32 + 28] = head
    hweight = z_head[...].astype(bf16)
    hrow = lax.broadcasted_iota(jnp.int32, (16, 128), 0)
    hlane = lax.broadcasted_iota(jnp.int32, (16, 128), 1)
    kind = lax.rem(hrow, 3)
    hbias = jnp.where(kind == 0, hb_ref[0], jnp.where(kind == 1, hb_ref[1], hb_ref[2]))
    depth = jnp.where((hrow < 3) | (hrow >= 9), bump(0, 4), bump(1, 4))
    wave = jnp.sin((hlane.astype(f32) + 0.5) * (math.pi / 128))
    window = depth * (wave * wave)

    def keep(a, v):
        b_feat[0:128, a * 128:(a + 1) * 128] = v.astype(bf16)

    layer(b_top, 0, 2, z_fourth, bo_ref, keep)
    settle()
    logits = jnp.dot(hweight, b_feat[0:128, :], preferred_element_type=f32)
    for a in range(12):
        value = jax.nn.sigmoid(logits[:, a * 128:(a + 1) * 128] + hbias) * (window * bump(a, 12))
        planes[pl.ds(3 + a, 12, stride=ROWS), :] = value[:12]


def kernel(feat, deep, wf, ws, wt, wo, bf_, bs, bt, bo, hw, hb, first_hbm, offset_hbm, out_ref,
           fbuf, dbuf, wfb, wsb, wtb, wob, bfb, bsb, btb, bob, hwb, hb_ref, first_ref, offset_ref,
           planes, plane, b_feat, b_mid, b_top, z_first, z_second, z_third, z_fourth, z_head,
           hot_ref, send_a, recv_a, pieces, send_b, recv_b, in_sem, sa_sem, ra_sem, sb_sem, rb_sem):
    seg = lax.axis_index("segment")
    patch = lax.axis_index("patch")
    half = lax.div(patch, 16)
    line = lax.rem(lax.div(patch, 4), 4)
    turn = lax.rem(patch, 4)
    here = half * 16 + turn * 4 + seg

    buffers = (fbuf, dbuf, wfb, wsb, wtb, wob, bfb, bsb, btb, bob, hwb)
    copies = copies_in(seg, (feat, deep, wf, ws, wt, wo, bf_, bs, bt, bo, hw), buffers, in_sem)
    tables = [pltpu.make_async_copy(src, dst, in_sem.at[11 + i]) for i, (src, dst) in enumerate(
        ((hb, hb_ref), (first_hbm, first_ref), (offset_hbm, offset_ref)))]
    for table in tables:
        table.start()

    halves = [half, 1 - half]
    turns = [lax.rem(turn + d, 4) for d in range(4)]
    segs = [lax.rem(seg + d, 4) for d in range(4)]
    lines = [lax.rem(line + d, 4) for d in range(4)]

    def device(h, y, t, s):
        return s * 32 + h * 16 + y * 4 + t

    others = [(h, t, s) for h in (1, 0) for t in (2, 1, 3, 0) for s in (2, 1, 3, 0) if h or t or s]
    ids = [device(halves[h], line, turns[t], segs[s]) for h, t, s in others]
    barrier = pltpu.get_barrier_semaphore()
    for peer in ids + [device(half, y, turn, seg) for y in lines[1:]]:
        pl.semaphore_signal(barrier, inc=1, device_id=peer, device_id_type=LOGICAL)

    def slots():
        for table in tables:
            table.wait()
        spot = lax.broadcasted_iota(jnp.int32, (32, 32), 1)
        rank = lax.broadcasted_iota(jnp.int32, (32, 32), 0)
        slot = jnp.zeros((32, 32), jnp.int32)
        for j in range(32):
            begin = first_ref[(j // 16 * 4 + line) * 16 + j % 16]
            block = begin + lax.rem(turn - begin + 256, 4)
            slot = jnp.where(spot == j, lax.div(block, 4), slot)
        goal = (rank % 8) * 8 + half * 4 + (rank // 8 + line) % 4
        hot_ref[...] = (slot == goal).astype(f32)

    convolve(copies, slots, buffers, hb_ref, planes, plane, b_feat, b_mid, b_top,
             z_first, z_second, z_third, z_fourth, z_head)

    own = patch * 4 + seg
    first = first_ref[own]
    shift = 3 - offset_ref[own]
    starts = [shift + 4 * lax.rem(t - first + 256, 4) for t in turns]
    pl.semaphore_wait(barrier, 34)

    def stage_a(n):
        h, t, s = others[n]
        return pltpu.make_async_remote_copy(
            src_ref=send_a.at[t * 4 + s], dst_ref=recv_a.at[here],
            send_sem=sa_sem, recv_sem=ra_sem,
            device_id=ids[n], device_id_type=LOGICAL)

    for n, (h, t, s) in enumerate(others):
        if h:
            base = segs[s] * (3 * ROWS) + starts[t]
            value = jnp.concatenate(
                [planes[pl.ds(base + kind * ROWS, 4), :] for kind in range(3)], axis=0)
            send_a[t * 4 + s] = (value * value).astype(bf16)
        stage_a(n).start()
    recv_a[here] = send_a[0]
    def all_pieces(ref, sem):
        return pltpu.make_async_copy(ref.at[pl.ds(0, 31)], ref.at[pl.ds(0, 31)], sem)

    all_pieces(recv_a, ra_sem).wait()

    for j in range(32):
        pieces[16 * j:16 * j + 12, :] = jnp.sqrt(recv_a[j].astype(f32))
    hot = hot_ref[...].astype(bf16)
    hot = jnp.concatenate([hot, hot], axis=1)
    for r in range(12):
        x = pieces[pl.ds(r, 32, stride=16), :]
        high = x.astype(bf16)
        low = (x - high.astype(f32)).astype(bf16)
        v = jnp.dot(hot, jnp.concatenate([high, low], axis=0), preferred_element_type=f32)
        v = v * v
        send_b[:, :, r * 128:(r + 1) * 128] = (v * v).reshape(4, 8, 128).astype(bf16)

    for d in (2, 1, 3):
        copy = pltpu.make_async_remote_copy(
            src_ref=send_b.at[d], dst_ref=recv_b.at[d],
            send_sem=sb_sem, recv_sem=rb_sem,
            device_id=device(half, lines[d], turn, seg), device_id_type=LOGICAL)
        copy.start()

    def decode(x):
        return jnp.sqrt(jnp.sqrt(x.astype(f32)))

    all_pieces(recv_a, sa_sem).wait()
    total = decode(send_b[0])
    pltpu.make_async_copy(recv_b.at[pl.ds(1, 3)], recv_b.at[pl.ds(1, 3)], rb_sem).wait()
    for d in range(1, 4):
        total = total + decode(recv_b[d])
    for r in range(12):
        out_ref[pl.ds(r, 8, stride=12), :] = total[:, r * 128:(r + 1) * 128]
    pltpu.make_async_copy(recv_b.at[pl.ds(1, 3)], recv_b.at[pl.ds(1, 3)], sb_sem).wait()


def conv_buffers():
    V = pltpu.VMEM
    return [
        V((1344, 128), bf16), V((1344, 128), bf16),
        V((9, 32, 28), bf16), V((27, 32, 28), bf16), V((27, 32, 56), bf16), V((27, 32, 56), bf16),
        V((1, 28), f32), V((1, 28), f32), V((1, 28), f32), V((1, 28), f32), V((3, 28), bf16),
    ]


def conv_scratch():
    V = pltpu.VMEM
    return [
        V((1536, 128), f32),
        V((384, 1536), bf16), V((768, 1536), bf16), V((768, 1536), bf16),
        V((384, 384), bf16), V((384, 384), bf16), V((384, 768), bf16), V((384, 768), bf16),
        V((16, 128), f32),
    ]


def per_device(features, deep_path, weight_first, bias_first, weight_second, bias_second,
               weight_third, bias_third, weight_fourth, bias_fourth, head_weight, head_bias,
               block_first, block_offset):
    def rows(x):
        return x.transpose(0, 1, 3, 2, 4).reshape(4, 1344, 128)

    hbm = pl.BlockSpec(memory_space=pltpu.HBM)
    vmem = pl.BlockSpec(memory_space=pltpu.VMEM)
    V = pltpu.VMEM
    dma = pltpu.SemaphoreType.DMA
    blended = pl.pallas_call(
        kernel,
        out_shape=V((96, 128), f32),
        in_specs=[hbm] * 14,
        out_specs=vmem,
        scratch_shapes=conv_buffers() + [
            pltpu.SMEM((3,), f32), pltpu.SMEM((128,), jnp.int32), pltpu.SMEM((128,), jnp.int32),
            V((12 * ROWS, 128), f32)] + conv_scratch() + [
            V((32, 32), f32), V((16, 12, 128), bf16), V((32, 12, 128), bf16), V((512, 128), f32),
            V((4, 8, 1536), bf16), V((4, 8, 1536), bf16),
            dma((14,)), dma(()), dma(()), dma(()), dma(()),
        ],
        compiler_params=pltpu.CompilerParams(
            collective_id=0, has_side_effects=True, vmem_limit_bytes=60 << 20),
    )(rows(features), rows(deep_path), weight_first, weight_second, weight_third, weight_fourth,
      bias_first.reshape(1, 28), bias_second.reshape(1, 28), bias_third.reshape(1, 28),
      bias_fourth.reshape(1, 28), head_weight, head_bias, block_first, block_offset)
    return blended.reshape(8, 1, 3, 1, 4, 128)


def solution(mesh):
    placed = (P("patch"), P("patch")) + (P(),) * 12
    return jax.shard_map(
        per_device,
        mesh=mesh,
        in_specs=placed,
        out_specs=P(None, "patch", None, "segment", None, None),
        check_vma=False,
    )
```

```python
import math

import jax
import jax.numpy as jnp
from jax import lax
from jax.experimental import pallas as pl
from jax.experimental.pallas import tpu as pltpu
from jax.sharding import PartitionSpec as P

bf16 = jnp.bfloat16
f32 = jnp.float32
LOGICAL = pl.DeviceIdType.LOGICAL
ROWS = 24


def bump(n, length):
    return math.sin(math.pi * (n + 0.5) / length) ** 2


def copies_in(s, hbm, buffers, sems):
    sources = [ref.at[s] if i < 2 else ref for i, ref in enumerate(hbm)]
    for w in buffers[2:6]:
        w[:, 16:32, :] = jnp.zeros((w.shape[0], 16, w.shape[2]), bf16)
    buffers = [w.at[:, 0:28, :] if 1 < i < 6 else w for i, w in enumerate(buffers)]
    copies = [pltpu.make_async_copy(src, dst, sems.at[i])
              for i, (src, dst) in enumerate(zip(sources, buffers))]
    for i in (2, 0, 6, 3, 7, 1, 4, 8, 5, 9, 10):
        copies[i].start()
    return copies


def convolve(copies, slots, buffers, hb_ref, planes, plane, b_feat, b_mid, b_top,
             z_first, z_second, z_third, z_fourth, z_head):
    fbuf, dbuf, wfb, wsb, wtb, wob, bf_ref, bs_ref, bt_ref, bo_ref, hw_ref = buffers

    plane[1344:1536, :] = jnp.zeros((192, 128), f32)
    planes[...] = jnp.zeros(planes.shape, f32)
    for dst in (z_first, z_second, z_third, z_fourth):
        dst[...] = jnp.zeros(dst.shape, bf16)
    lane = lax.broadcasted_iota(jnp.int32, (128, 128), 1)

    def put(buf, row0, col0, v):
        v = v.astype(bf16)
        zero = jnp.zeros((128, 128), bf16)
        buf[row0:row0 + 128, col0:col0 + 128] = jnp.where(lane > 0, pltpu.roll(v, 1, 1), zero)
        buf[row0 + 128:row0 + 256, col0:col0 + 128] = v
        buf[row0 + 256:row0 + 384, col0:col0 + 128] = jnp.where(lane < 127, pltpu.roll(v, 127, 1), zero)

    def relayout(src, buf, row0):
        for c in range(0, 1344, 336):
            plane[c:c + 336, :] = src[c:c + 336, :].astype(f32)
            yield
        for a in range(12):
            cell = [plane[pl.ds(4 * a + z, 32, stride=48), :] for z in range(4)]
            put(buf, row0, a * 128, jnp.concatenate(cell, axis=0))
            yield

    def expand(w, dst, parts, full):
        for t in range(9):
            da, dy = t // 3, t % 3
            for part in range(parts):
                base = (part * 3 + dy) * 128
                for zo in range(4):
                    for zi in range(4):
                        if abs(zi - zo) > (1 if full else 0):
                            continue
                        tap = 9 * (zi - zo + 1) + t if full else t
                        dst[da * 128 + zo * 32:da * 128 + zo * 32 + 32, base + zi * 32:base + zi * 32 + 28] = (
                            w[tap, :, part * 28:part * 28 + 28])
                yield

    def column(ref):
        lanes = lax.broadcasted_iota(jnp.int32, (128, 28), 1)
        rows = lax.rem(lax.broadcasted_iota(jnp.int32, (128, 28), 0), 32)
        return jnp.sum(jnp.where(lanes == rows, ref[...], 0.0), axis=1, keepdims=True)

    def layer(src, row0, parts, weights, bias_ref, emit, beside=()):
        k = parts * 384
        bias = column(bias_ref)
        sums = {}
        for n in range(6):
            p = jnp.dot(weights[...], src[row0:row0 + k, n * 256:(n + 1) * 256],
                        preferred_element_type=f32)
            for task, count in beside:
                for _ in range(count):
                    next(task, None)
            settle()
            for b in (2 * n, 2 * n + 1):
                for da in (2, 1, 0):
                    a = b + 1 - da
                    if 0 <= a < 12:
                        term = p[da * 128:(da + 1) * 128, (b - 2 * n) * 128:(b - 2 * n + 1) * 128]
                        sums[a] = sums[a] + term if a in sums else term
            for a in (2 * n - 1, 2 * n) + ((11,) if n == 5 else ()):
                if a >= 0:
                    pending.append((emit, a, sums.pop(a), bias))

    pending = []

    def settle():
        while pending:
            emit, a, total, bias = pending.pop(0)
            emit(a, jnp.maximum(total + bias, 0.0))

    def run(task):
        for _ in task:
            pass

    copies[2].wait()
    run(expand(wfb, z_first, 1, False))
    copies[0].wait()
    run(relayout(fbuf, b_feat, 0))
    slots()
    for i in (6, 3, 7, 1, 4, 8, 5, 9, 10):
        copies[i].wait()
    second = expand(wsb, z_second, 1, True)
    deeper = relayout(dbuf, b_mid, 384)
    layer(b_feat, 0, 1, z_first, bf_ref, lambda a, v: put(b_top, 384, a * 128, v), [(second, 2), (deeper, 2)])
    run(second)
    third = expand(wtb, z_third, 2, True)
    fourth = expand(wob, z_fourth, 2, True)
    layer(b_top, 384, 1, z_second, bs_ref, lambda a, v: put(b_mid, 0, a * 128, v), [(deeper, 3), (third, 3)])
    run(deeper)
    run(third)
    layer(b_mid, 0, 2, z_third, bt_ref, lambda a, v: put(b_top, 0, a * 128, v), [(fourth, 3)])
    run(fourth)

    z_head[...] = jnp.zeros((16, 128), f32)
    head = hw_ref[...].astype(f32)
    for z in range(4):
        z_head[z * 3:z * 3 + 3, z * 32:z * 32 + 28] = head
    hweight = z_head[...].astype(bf16)
    hrow = lax.broadcasted_iota(jnp.int32, (16, 128), 0)
    hlane = lax.broadcasted_iota(jnp.int32, (16, 128), 1)
    kind = lax.rem(hrow, 3)
    hbias = jnp.where(kind == 0, hb_ref[0], jnp.where(kind == 1, hb_ref[1], hb_ref[2]))
    depth = jnp.where((hrow < 3) | (hrow >= 9), bump(0, 4), bump(1, 4))
    wave = jnp.sin((hlane.astype(f32) + 0.5) * (math.pi / 128))
    window = depth * (wave * wave)

    def keep(a, v):
        b_feat[0:128, a * 128:(a + 1) * 128] = v.astype(bf16)

    layer(b_top, 0, 2, z_fourth, bo_ref, keep)
    settle()
    logits = jnp.dot(hweight, b_feat[0:128, :], preferred_element_type=f32)
    for a in range(12):
        value = jax.nn.sigmoid(logits[:, a * 128:(a + 1) * 128] + hbias) * (window * bump(a, 12))
        planes[pl.ds(3 + a, 12, stride=ROWS), :] = value[:12]


def kernel(feat, deep, wf, ws, wt, wo, bf_, bs, bt, bo, hw, hb, first_hbm, offset_hbm, out_ref,
           fbuf, dbuf, wfb, wsb, wtb, wob, bfb, bsb, btb, bob, hwb, hb_ref, first_ref, offset_ref,
           planes, plane, b_feat, b_mid, b_top, z_first, z_second, z_third, z_fourth, z_head,
           hot_ref, send_a, recv_a, pieces, send_b, recv_b, in_sem, sa_sem, ra_sem, sb_sem, rb_sem):
    seg = lax.axis_index("segment")
    patch = lax.axis_index("patch")
    half = lax.div(patch, 16)
    line = lax.rem(lax.div(patch, 4), 4)
    turn = lax.rem(patch, 4)
    here = half * 16 + turn * 4 + seg

    buffers = (fbuf, dbuf, wfb, wsb, wtb, wob, bfb, bsb, btb, bob, hwb)
    copies = copies_in(seg, (feat, deep, wf, ws, wt, wo, bf_, bs, bt, bo, hw), buffers, in_sem)
    tables = [pltpu.make_async_copy(src, dst, in_sem.at[11 + i]) for i, (src, dst) in enumerate(
        ((hb, hb_ref), (first_hbm, first_ref), (offset_hbm, offset_ref)))]
    for table in tables:
        table.start()

    halves = [half, 1 - half]
    turns = [lax.rem(turn + d, 4) for d in range(4)]
    segs = [lax.rem(seg + d, 4) for d in range(4)]
    lines = [lax.rem(line + d, 4) for d in range(4)]

    def device(h, y, t, s):
        return s * 32 + h * 16 + y * 4 + t

    others = [(h, t, s) for h in (1, 0) for t in (2, 1, 3, 0) for s in (2, 1, 3, 0) if h or t or s]
    ids = [device(halves[h], line, turns[t], segs[s]) for h, t, s in others]
    barrier = pltpu.get_barrier_semaphore()
    for peer in ids + [device(half, y, turn, seg) for y in lines[1:]]:
        pl.semaphore_signal(barrier, inc=1, device_id=peer, device_id_type=LOGICAL)

    def slots():
        for table in tables:
            table.wait()
        spot = lax.broadcasted_iota(jnp.int32, (32, 32), 1)
        rank = lax.broadcasted_iota(jnp.int32, (32, 32), 0)
        slot = jnp.zeros((32, 32), jnp.int32)
        for j in range(32):
            begin = first_ref[(j // 16 * 4 + line) * 16 + j % 16]
            block = begin + lax.rem(turn - begin + 256, 4)
            slot = jnp.where(spot == j, lax.div(block, 4), slot)
        goal = (rank % 8) * 8 + half * 4 + (rank // 8 + line) % 4
        hot_ref[...] = (slot == goal).astype(f32)

    convolve(copies, slots, buffers, hb_ref, planes, plane, b_feat, b_mid, b_top,
             z_first, z_second, z_third, z_fourth, z_head)

    own = patch * 4 + seg
    first = first_ref[own]
    shift = 3 - offset_ref[own]
    starts = [shift + 4 * lax.rem(t - first + 256, 4) for t in turns]
    pl.semaphore_wait(barrier, 34)

    def stage_a(n):
        h, t, s = others[n]
        return pltpu.make_async_remote_copy(
            src_ref=send_a.at[t * 4 + s], dst_ref=recv_a.at[here],
            send_sem=sa_sem, recv_sem=ra_sem,
            device_id=ids[n], device_id_type=LOGICAL)

    for n, (h, t, s) in enumerate(others):
        if h:
            base = segs[s] * (3 * ROWS) + starts[t]
            value = jnp.concatenate(
                [planes[pl.ds(base + kind * ROWS, 4), :] for kind in range(3)], axis=0)
            send_a[t * 4 + s] = (value * value).astype(bf16)
        stage_a(n).start()
    recv_a[here] = send_a[0]
    def all_pieces(ref, sem):
        return pltpu.make_async_copy(ref.at[pl.ds(0, 31)], ref.at[pl.ds(0, 31)], sem)

    all_pieces(recv_a, ra_sem).wait()

    for j in range(32):
        pieces[16 * j:16 * j + 12, :] = jnp.sqrt(recv_a[j].astype(f32))
    hot = hot_ref[...].astype(bf16)
    hot = jnp.concatenate([hot, hot], axis=1)
    x = jnp.concatenate([pieces[pl.ds(r, 32, stride=16), :] for r in range(12)], axis=1)
    high = x.astype(bf16)
    low = (x - high.astype(f32)).astype(bf16)
    v = jnp.dot(hot, jnp.concatenate([high, low], axis=0), preferred_element_type=f32)
    v = v * v
    send_b[...] = (v * v).reshape(4, 8, 1536).astype(bf16)

    for d in (2, 1, 3):
        copy = pltpu.make_async_remote_copy(
            src_ref=send_b.at[d], dst_ref=recv_b.at[d],
            send_sem=sb_sem, recv_sem=rb_sem,
            device_id=device(half, lines[d], turn, seg), device_id_type=LOGICAL)
        copy.start()

    def decode(x):
        return jnp.sqrt(jnp.sqrt(x.astype(f32)))

    all_pieces(recv_a, sa_sem).wait()
    total = decode(send_b[0])
    pltpu.make_async_copy(recv_b.at[pl.ds(1, 3)], recv_b.at[pl.ds(1, 3)], rb_sem).wait()
    for d in range(1, 4):
        total = total + decode(recv_b[d])
    for r in range(12):
        out_ref[pl.ds(r, 8, stride=12), :] = total[:, r * 128:(r + 1) * 128]
    pltpu.make_async_copy(recv_b.at[pl.ds(1, 3)], recv_b.at[pl.ds(1, 3)], sb_sem).wait()


def conv_buffers():
    V = pltpu.VMEM
    return [
        V((1344, 128), bf16), V((1344, 128), bf16),
        V((9, 32, 28), bf16), V((27, 32, 28), bf16), V((27, 32, 56), bf16), V((27, 32, 56), bf16),
        V((1, 28), f32), V((1, 28), f32), V((1, 28), f32), V((1, 28), f32), V((3, 28), bf16),
    ]


def conv_scratch():
    V = pltpu.VMEM
    return [
        V((1536, 128), f32),
        V((384, 1536), bf16), V((768, 1536), bf16), V((768, 1536), bf16),
        V((384, 384), bf16), V((384, 384), bf16), V((384, 768), bf16), V((384, 768), bf16),
        V((16, 128), f32),
    ]


def per_device(features, deep_path, weight_first, bias_first, weight_second, bias_second,
               weight_third, bias_third, weight_fourth, bias_fourth, head_weight, head_bias,
               block_first, block_offset):
    def rows(x):
        return x.transpose(0, 1, 3, 2, 4).reshape(4, 1344, 128)

    hbm = pl.BlockSpec(memory_space=pltpu.HBM)
    vmem = pl.BlockSpec(memory_space=pltpu.VMEM)
    V = pltpu.VMEM
    dma = pltpu.SemaphoreType.DMA
    blended = pl.pallas_call(
        kernel,
        out_shape=V((96, 128), f32),
        in_specs=[hbm] * 14,
        out_specs=vmem,
        scratch_shapes=conv_buffers() + [
            pltpu.SMEM((3,), f32), pltpu.SMEM((128,), jnp.int32), pltpu.SMEM((128,), jnp.int32),
            V((12 * ROWS, 128), f32)] + conv_scratch() + [
            V((32, 32), f32), V((16, 12, 128), bf16), V((32, 12, 128), bf16), V((512, 128), f32),
            V((4, 8, 1536), bf16), V((4, 8, 1536), bf16),
            dma((14,)), dma(()), dma(()), dma(()), dma(()),
        ],
        compiler_params=pltpu.CompilerParams(
            collective_id=0, has_side_effects=True, vmem_limit_bytes=60 << 20),
    )(rows(features), rows(deep_path), weight_first, weight_second, weight_third, weight_fourth,
      bias_first.reshape(1, 28), bias_second.reshape(1, 28), bias_third.reshape(1, 28),
      bias_fourth.reshape(1, 28), head_weight, head_bias, block_first, block_offset)
    return blended.reshape(8, 1, 3, 1, 4, 128)


def solution(mesh):
    placed = (P("patch"), P("patch")) + (P(),) * 12
    return jax.shard_map(
        per_device,
        mesh=mesh,
        in_specs=placed,
        out_specs=P(None, "patch", None, "segment", None, None),
        check_vma=False,
    )
```
